256 devices in a mesh: morton: 64 (over y, x_hi, z), sub: 4 (over x_lo, core).
Axes of the slice: x: 4 (x_hi: 2, x_lo: 2; x = x_hi * 2 + x_lo), y: 4, z: 8, core: 2. Of those that a mesh axis runs over, the one named last changes fastest.
Arguments:
- multipoles: bfloat16 [16384, 128], P(('morton', 'sub')), may hold values from -6 to 6
- translations: bfloat16 [316, 128, 128], P('sub'), may hold values from -0.0625 to 0.0625
- upward_ops: bfloat16 [8, 128, 128], replicated, may hold values from -0.1875 to 0.1875
- downward_ops: bfloat16 [8, 128, 128], replicated, may hold values from -0.375 to 0.375
- targets_l6: int32 [64, 316, 128], P('morton', 'sub'), may hold values from 0 to 255, as said below
- source_boxes_level6: int32 [64, 316, 128], P('morton', 'sub'), may hold values from 0 to 767, as said below
- counts_l6: int32 [64, 316], P('morton', 'sub'), may hold values from 1 to 128, as said below
- target_boxes_level5: int32 [64, 316, 16], P('morton', 'sub'), may hold values from 0 to 31, as said below
- anchors_l5: int32 [64, 316, 16], P('morton', 'sub'), may hold values from 0 to 255, as said below
- counts_l5: int32 [64, 316], P('morton', 'sub'), may hold values from 1 to 16, as said below
- targets_l4: int32 [64, 316, 2], P('morton', 'sub'), may hold values from 0 to 3, as said below
- anchors_l4: int32 [64, 316, 2], P('morton', 'sub'), may hold values from 0 to 31, as said below
- counts_l4: int32 [64, 316], P('morton', 'sub'), may hold values from 1 to 2, as said below
Outputs:
- local_exp: bfloat16 [16384, 128], P(('morton', 'sub'))
The draws below stay inside these ranges and needn't reach their ends.
Inputs may be any that keep to these rules, and one draw needn't show every extreme that they name: `targets_l6`: targets of one operator's block within one subtree are its level-6 boxes. `source_boxes_level6`: sources lie in the previous, own or next subtree, at most 256 boxes before or after the target. `counts_l6`: some block of every subtree is full. `target_boxes_level5`: targets are level-5 boxes of the subtree. `anchors_l5`: sources are level-5 boxes of the aligned group of 8 subtrees. `counts_l5`: some block of every subtree is full. `targets_l4`: targets are level-4 boxes of the subtree. `anchors_l4`: sources are level-4 boxes of the aligned group of 8 subtrees. `counts_l4`: some block of every subtree is full.
All inputs are finite; a program needn't handle non-finite values.
Results may differ from the reference program's by a relative error of at most 0.011.
Values may be sent and summed in bfloat16 or wider, within the bound.
No kernel may reach another device: no remote copies, remote signals or barrier semaphores. Data moves between devices by JAX's collectives and lax.ppermute only.
A program may use at most 64 MiB of HBM per device.

```python
import jax
import jax.numpy as jnp
from jax import lax

R = 128
NOPS = 316
B6M = 256
SUBTREES = 64
B5M = 32
B4M = 4
CAP6 = 128
CAP5 = 16
CAP4 = 2
NB6 = 16384
N_SUB = 4


def pair_tables(key, box_count, capacity, level_tag, halo_space):
    key = jax.random.fold_in(key, level_tag)
    key_list = jax.random.split(key, 6)
    table_shape = (SUBTREES, NOPS, capacity)
    chosen = jax.random.randint(key_list[4], (SUBTREES, 1), 0, NOPS)
    is_chosen = jnp.arange(NOPS, dtype=jnp.int32)[None, :] == chosen
    chosen_block = is_chosen[:, :, None]
    begins = jax.random.randint(key_list[0], (SUBTREES, NOPS, 1), 0, box_count)
    begins = jnp.where(chosen_block, box_count - 1, begins)
    strides = 2 * jax.random.randint(key_list[1], (SUBTREES, NOPS, 1), 0, max(box_count // 2, 1)) + 1
    strides = jnp.where(chosen_block, 1, strides)
    slot_numbers = jnp.arange(capacity, dtype=jnp.int32)[None, None, :]
    targets = (begins + strides * slot_numbers) % box_count
    leading_slot = jnp.logical_and(chosen_block, slot_numbers == 0)
    second_slot = jnp.logical_and(chosen_block, slot_numbers == 1)
    if halo_space:
        offsets = jax.random.randint(key_list[2], table_shape, 0, 2 * box_count + 1)
        offsets = jnp.where(leading_slot, 2 * box_count, jnp.where(second_slot, 0, offsets))
        anchors = targets + offsets
    else:
        anchors = jax.random.randint(key_list[2], table_shape, 0, 8 * box_count)
        anchors = jnp.where(leading_slot, 8 * box_count - 1, jnp.where(second_slot, 0, anchors))
    filled = jax.random.randint(key_list[3], (SUBTREES, NOPS), 0, 7) == 0
    filled = jnp.logical_or(filled, is_chosen)
    counts = jnp.where(filled, capacity, jax.random.randint(key_list[5], (SUBTREES, NOPS), 1, capacity + 1))
    return (targets.astype(jnp.int32), anchors.astype(jnp.int32), counts.astype(jnp.int32))


def draw_targets_l6(key, part):
    return pair_tables(key, B6M, CAP6, 6, True)[0]


def draw_source_boxes_level6(key, part):
    return pair_tables(key, B6M, CAP6, 6, True)[1]


def draw_counts_l6(key, part):
    return pair_tables(key, B6M, CAP6, 6, True)[2]


def draw_target_boxes_level5(key, part):
    return pair_tables(key, B5M, CAP5, 5, False)[0]


def draw_anchors_l5(key, part):
    return pair_tables(key, B5M, CAP5, 5, False)[1]


def draw_counts_l5(key, part):
    return pair_tables(key, B5M, CAP5, 5, False)[2]


def draw_targets_l4(key, part):
    return pair_tables(key, B4M, CAP4, 4, False)[0]


def draw_anchors_l4(key, part):
    return pair_tables(key, B4M, CAP4, 4, False)[1]


def draw_counts_l4(key, part):
    return pair_tables(key, B4M, CAP4, 4, False)[2]


def block_levels(key, shape, shards, least, largest):
    def one(dim, blocks):
        steps = jax.random.uniform(jax.random.fold_in(jax.random.fold_in(key, 6), dim), (blocks,), jnp.float32, least / len(shards), largest / len(shards))
        return jnp.repeat(jnp.exp(steps), shape[dim] // blocks).reshape((-1,) + (1,) * (len(shape) - dim - 1))

    factor_of = one(*shards[0])
    for cut in shards[1:]:
        factor_of = factor_of * one(*cut)
    return factor_of


def centred(rng, extent, scale, limit, cuts=(), kind=jnp.bfloat16):
    loudness = block_levels(rng, extent, cuts, -0.22, 0.18) if cuts else 1.0
    entries = jax.random.normal(rng, extent, jnp.float32) * scale * loudness
    return jnp.minimum(jnp.maximum(entries, -limit), limit).astype(kind)


def setup_inputs(seed: int = 0) -> dict:
    seeds = jax.random.split(jax.random.key(seed), 14)
    multipoles = centred(seeds[0], (NB6, R), 1.0, 6.0, ((0, 256),))
    translations = centred(seeds[1], (NOPS, R, R), (64 * R) ** -0.5, 0.0625, ((0, 4),))
    upward_ops = centred(seeds[2], (8, R, R), (8 * R) ** -0.5, 0.1875)
    downward_ops = centred(seeds[3], (8, R, R), (2 * R) ** -0.5, 0.375)
    targets_l6 = draw_targets_l6(jax.random.fold_in(seeds[13], 71), 0)
    source_boxes_level6 = draw_source_boxes_level6(jax.random.fold_in(seeds[13], 71), 0)
    counts_l6 = draw_counts_l6(jax.random.fold_in(seeds[13], 71), 0)
    target_boxes_level5 = draw_target_boxes_level5(jax.random.fold_in(seeds[13], 71), 0)
    anchors_l5 = draw_anchors_l5(jax.random.fold_in(seeds[13], 71), 0)
    counts_l5 = draw_counts_l5(jax.random.fold_in(seeds[13], 71), 0)
    targets_l4 = draw_targets_l4(jax.random.fold_in(seeds[13], 71), 0)
    anchors_l4 = draw_anchors_l4(jax.random.fold_in(seeds[13], 71), 0)
    counts_l4 = draw_counts_l4(jax.random.fold_in(seeds[13], 71), 0)
    return dict(multipoles=multipoles, translations=translations, upward_ops=upward_ops, downward_ops=downward_ops, targets_l6=targets_l6, source_boxes_level6=source_boxes_level6, counts_l6=counts_l6, target_boxes_level5=target_boxes_level5, anchors_l5=anchors_l5, counts_l5=counts_l5, targets_l4=targets_l4, anchors_l4=anchors_l4, counts_l4=counts_l4)


def translate_block(expansions, targets, anchors, counts, kernels, row_count, factor):
    operator_matrices, capacity = targets.shape
    coeff_width = expansions.shape[1]
    block_rows = min(capacity, 128)
    turn_count = capacity // block_rows
    target_steps = targets.reshape(operator_matrices, turn_count, block_rows).transpose(1, 0, 2)
    anchor_steps = anchors.reshape(operator_matrices, turn_count, block_rows).transpose(1, 0, 2)
    slot_steps = jnp.arange(capacity, dtype=jnp.int32).reshape(turn_count, block_rows)
    wide_kernels = kernels.astype(jnp.float32)

    def single_rotation(totals, inputs):
        target_rows, anchor_rows, slot_numbers = inputs
        picked = expansions[anchor_rows].astype(jnp.float32)
        product = jnp.einsum("obr,ors->obs", picked, wide_kernels, precision=lax.Precision.HIGHEST)
        is_live = slot_numbers[None, :] < counts[:, None]
        product = jnp.where(is_live[:, :, None], product, 0.0) * factor
        return totals.at[target_rows.reshape(-1)].add(product.reshape(-1, coeff_width)), None

    totals, _ = lax.scan(single_rotation, jnp.zeros((row_count, coeff_width), jnp.float32), (target_steps, anchor_steps, slot_steps))
    return totals


def upward(children, operator_matrices):
    parents = children.shape[0] // 8
    grouped_rows = children.reshape(parents, 8, children.shape[1]).astype(jnp.float32)
    summed_values = jnp.einsum("duo,uob->db", grouped_rows, operator_matrices.astype(jnp.float32), precision=lax.Precision.HIGHEST)
    return summed_values.astype(jnp.bfloat16)


def downward(parent, operator_matrices):
    spread = jnp.einsum("pr,crs->pcs", parent.astype(jnp.float32), operator_matrices.astype(jnp.float32), precision=lax.Precision.HIGHEST)
    return spread.reshape(-1, parent.shape[1])


def reference(multipoles, translations, upward_ops, downward_ops, targets_l6, source_boxes_level6, counts_l6, target_boxes_level5, anchors_l5, counts_l5, targets_l4, anchors_l4, counts_l4):
    coeff_width = multipoles.shape[1]
    blank = jnp.zeros((B6M, coeff_width), jnp.bfloat16)
    padded = jnp.concatenate([blank, multipoles, blank], axis=0)
    coarse5 = upward(multipoles, upward_ops)
    coarse4 = upward(coarse5, upward_ops)
    subtree_ids = jnp.arange(SUBTREES, dtype=jnp.int32)
    group_size = NOPS // N_SUB

    def level_six(subtree):
        nearby = lax.dynamic_slice_in_dim(padded, subtree * B6M, 3 * B6M, 0)
        total = jnp.zeros((B6M, coeff_width), jnp.float32)
        for group in range(N_SUB):
            first = group * group_size
            last = first + group_size
            partial_value = translate_block(nearby, targets_l6[subtree, first:last], source_boxes_level6[subtree, first:last], counts_l6[subtree, first:last], translations[first:last], B6M, 1.0)
            rounded = lax.optimization_barrier(partial_value.astype(jnp.bfloat16))
            total = total + rounded.astype(jnp.float32)
        return total

    def level_five(subtree):
        group_rows = lax.dynamic_slice_in_dim(coarse5, (subtree // 8) * (8 * B5M), 8 * B5M, 0)
        return translate_block(group_rows, target_boxes_level5[subtree], anchors_l5[subtree], counts_l5[subtree], translations, B5M, 0.5)

    def level_four(subtree):
        group_rows = lax.dynamic_slice_in_dim(coarse4, (subtree // 8) * (8 * B4M), 8 * B4M, 0)
        return translate_block(group_rows, targets_l4[subtree], anchors_l4[subtree], counts_l4[subtree], translations, B4M, 0.25)

    far_six = lax.map(level_six, subtree_ids).reshape(-1, coeff_width)
    far_five = lax.map(level_five, subtree_ids).reshape(-1, coeff_width)
    far_four = lax.map(level_four, subtree_ids).reshape(-1, coeff_width)
    local4 = far_four.astype(jnp.bfloat16)
    local5 = (far_five + downward(local4, downward_ops)).astype(jnp.bfloat16)
    return (far_six + downward(local5, downward_ops)).astype(jnp.bfloat16)
```

```python
import jax
import jax.numpy as jnp
from jax import lax
from jax.experimental import pallas as pl
from jax.experimental.pallas import tpu as pltpu
from jax.sharding import Mesh
from jax.sharding import PartitionSpec as P

R = 128
NO = 79
G = 4
BF = jnp.bfloat16
F32 = jnp.float32


def iota(shape, dim):
    return lax.broadcasted_iota(jnp.int32, shape, dim)


def prep_kernel(q_ref, m_ref, up_ref, src_ref, c6_ref, a5_ref, c5_ref, a4_ref, c4_ref, t5_ref, t4_ref,
                grp_ref, low6_ref, hi6_ref, low54_ref, hi54_ref, t54_ref, sq_ref, st_ref):
    q = q_ref[0]
    st_ref[pl.ds(0, 64), :] = m_ref[...].astype(F32)
    c5 = jnp.zeros((8, R), F32)
    for c in range(8):
        rows = st_ref[pl.ds(c, 8, stride=8), :].astype(BF)
        c5 = c5 + jnp.dot(rows, up_ref[c], preferred_element_type=F32)
    c5r = c5.astype(BF).astype(F32)
    c4 = jnp.zeros((8, R), F32)
    for c in range(8):
        rows = jnp.broadcast_to(c5r[c : c + 1, :], (8, R)).astype(BF)
        c4 = c4 + jnp.dot(rows, up_ref[c], preferred_element_type=F32)
    both = jnp.concatenate([c5, c4], axis=0).astype(BF)
    grp_ref[...] = jnp.broadcast_to(both[None], (32, 16, R))

    def flipped(x):
        sq_ref[...] = jnp.zeros((R, R), F32)
        sq_ref[0:NO, 0 : x.shape[1]] = x.astype(F32)
        return sq_ref[...].T

    def live(c_ref, rows):
        sq_ref[0:1, :] = jnp.zeros((1, R), F32)
        sq_ref[0:1, 0:NO] = c_ref[...].astype(F32)
        counts = jnp.broadcast_to(sq_ref[0:1, :], (rows, R))
        return iota((rows, R), 0).astype(F32) < counts

    src = src_ref[...]
    low = flipped(jnp.bitwise_xor(jnp.bitwise_and(src, 255), q * 64))
    hi = flipped(jnp.right_shift(src, 8))
    low6_ref[...] = jnp.where(live(c6_ref, R), low, -1.0)
    hi6_ref[...] = hi
    a5 = a5_ref[...]
    code5 = flipped(16 * jnp.right_shift(a5, 3) + jnp.bitwise_and(a5, 7))[0:16]
    code5 = jnp.where(live(c5_ref, 16), code5, -1.0)
    code4 = flipped(16 * a4_ref[...] + 8)[0:16]
    code4 = jnp.where(live(c4_ref, 16), code4, -1.0)
    code = jnp.concatenate([code5, code4], axis=0)
    upper = code >= 256.0
    low54_ref[...] = jnp.where(upper, code - 256.0, code)
    hi54_ref[...] = upper.astype(F32)
    sq_ref[...] = jnp.full((R, R), -1.0, F32)
    sq_ref[0:NO, 0:16] = t5_ref[...].astype(F32)
    sq_ref[0:NO, 16:18] = t4_ref[...].astype(F32) + 32.0
    packed = sq_ref[pl.ds(0, 24, stride=4), :]
    lane = iota((24, R), 1)
    for i in range(1, G):
        part = pltpu.roll(sq_ref[pl.ds(i, 24, stride=4), :], 32 * i, 1)
        packed = jnp.where(lane >= 32 * i, part, packed)
    t54_ref[...] = packed


def main_kernel(q_ref, own_ref, prev_ref, next_ref, grp_ref, t_ref, low6_ref, hi6_ref, low54_ref, hi54_ref,
                tgt_ref, t54_ref, o0_ref, o1_ref, o2_ref, o3_ref, x_ref, x54_ref, acc_ref, acc54_ref, tf_ref):
    x_ref[:, 0:R] = prev_ref[...]
    x_ref[:, R : 2 * R] = own_ref[...]
    x_ref[:, 2 * R : 3 * R] = next_ref[...]
    x54_ref[:, 0:R] = grp_ref[0:16].reshape(256, R)
    x54_ref[:, R : 2 * R] = grp_ref[16:32].reshape(256, R)
    acc_ref[...] = jnp.zeros_like(acc_ref)
    acc54_ref[...] = jnp.zeros_like(acc54_ref)
    tf_ref[0:NO, :] = tgt_ref[...].astype(F32)

    def hot(column, rows):
        wide = jnp.broadcast_to(column, (rows, R)).astype(BF)
        lane = iota((rows, R), 1).astype(BF)
        one = jnp.ones((rows, R), BF)
        zero = jnp.zeros((rows, R), BF)
        left = jnp.where(wide == lane, one, zero)
        right = jnp.where(wide == lane + jnp.asarray(128, BF), one, zero)
        return jnp.concatenate([left, right], axis=1)

    def placing(row, rows, base):
        wide = jnp.broadcast_to(row, (rows, R)).astype(BF)
        down = (iota((rows, R), 0) + base).astype(BF)
        return jnp.where(wide == down, jnp.ones((rows, R), BF), jnp.zeros((rows, R), BF))

    def group(g, count):
        first = g * G
        shift = lax.rem(R - first, R)
        low6 = pltpu.roll(low6_ref[...], shift, 1)
        hi6 = pltpu.roll(hi6_ref[...], shift, 1)
        low54 = pltpu.roll(low54_ref[...], shift, 1)
        hi54 = pltpu.roll(hi54_ref[...], shift, 1)
        ys, y54s, places = [], [], []
        for i in range(count):
            picked = jnp.dot(hot(low6[:, i : i + 1], R), x_ref[...], preferred_element_type=F32)
            seg = jnp.broadcast_to(hi6[:, i : i + 1], (R, R))
            picked = jnp.where(seg == 0.0, picked[:, 0:R], jnp.where(seg == 1.0, picked[:, R : 2 * R], picked[:, 2 * R :]))
            few = jnp.dot(hot(low54[:, i : i + 1], 32), x54_ref[...], preferred_element_type=F32)
            seg = jnp.broadcast_to(hi54[:, i : i + 1], (32, R))
            few = jnp.where(seg == 0.0, few[:, 0:R], few[:, R:])
            rows = jnp.concatenate([picked.astype(BF), few.astype(BF)], axis=0)
            y = jnp.dot(rows, t_ref[first + i], preferred_element_type=F32).astype(BF)
            ys.append(y[0:R])
            y54s.append(y[R:])
            places.append(placing(tf_ref[pl.ds(first + i, 1), :], 256, 0))
        acc_ref[...] += jnp.dot(jnp.concatenate(places, axis=1), jnp.concatenate(ys, axis=0), preferred_element_type=F32)
        if count < G:
            y54s.append(jnp.zeros((32 * (G - count), R), BF))
        acc54_ref[...] += jnp.dot(placing(t54_ref[pl.ds(g, 1), :], 48, 0), jnp.concatenate(y54s, axis=0), preferred_element_type=F32)

    def body(g, carry):
        group(g, G)
        return carry

    lax.fori_loop(0, NO // G, body, 0)
    group(NO // G, NO % G)
    q = q_ref[0]
    acc54_ref[0:32] = acc54_ref[0:32] * 0.5
    acc54_ref[32:48] = acc54_ref[32:48] * 0.25
    for k, out in enumerate((o0_ref, o1_ref, o2_ref, o3_ref)):
        d = jnp.bitwise_xor(q, k)
        out[0:64] = acc_ref[pl.ds(64 * d, 64), :].astype(BF)
        five = acc54_ref[pl.ds(8 * d, 8), :]
        four = jnp.broadcast_to(acc54_ref[pl.ds(32 + d, 1), :], (8, R))
        small = jnp.concatenate([five, four], axis=0)
        top = small.astype(BF)
        out[64:80] = top
        out[80:96] = (small - top.astype(F32)).astype(BF)


def final_kernel(a_ref, b_ref, c_ref, d_ref, dn_ref, out_ref, s_ref):
    total = (a_ref[...].astype(F32) + b_ref[...].astype(F32)) + (c_ref[...].astype(F32) + d_ref[...].astype(F32))
    small = total[64:80] + total[80:96]
    far5 = small[0:8]
    local4 = small[8:16].astype(BF)
    row = iota((8, R), 0)
    local5 = far5
    for c in range(8):
        spread = jnp.dot(local4, dn_ref[c], preferred_element_type=F32)
        local5 = local5 + jnp.where(row == c, spread, 0.0)
    local5 = local5.astype(BF)
    for c in range(8):
        s_ref[pl.ds(c, 8, stride=8), :] = jnp.dot(local5, dn_ref[c], preferred_element_type=F32)
    out_ref[...] = (total[0:64] + s_ref[...]).astype(BF)


VM = pl.BlockSpec(memory_space=pltpu.VMEM)
SM = pl.BlockSpec(memory_space=pltpu.SMEM)


def shape(dims, kind=F32):
    return jax.ShapeDtypeStruct(dims, kind)


def run_prep(q, *args):
    return pl.pallas_call(
        prep_kernel,
        out_shape=(shape((32, 16, R), BF), shape((R, R)), shape((R, R)), shape((32, R)), shape((32, R)), shape((24, R))),
        in_specs=[SM] + [VM] * len(args),
        out_specs=tuple([VM] * 6),
        scratch_shapes=[pltpu.VMEM((R, R), F32), pltpu.VMEM((64, R), F32)],
        name="prep",
    )(q, *args)


def run_main(q, *args):
    return pl.pallas_call(
        main_kernel,
        out_shape=tuple([shape((96, R), BF)] * 4),
        in_specs=[SM] + [VM] * len(args),
        out_specs=tuple([VM] * 4),
        scratch_shapes=[
            pltpu.VMEM((256, 3 * R), BF),
            pltpu.VMEM((256, 2 * R), BF),
            pltpu.VMEM((256, R), F32),
            pltpu.VMEM((48, R), F32),
            pltpu.VMEM((80, R), F32),
        ],
        name="translate",
    )(q, *args)


def run_final(*args):
    return pl.pallas_call(
        final_kernel,
        out_shape=shape((64, R), BF),
        in_specs=[VM] * len(args),
        out_specs=VM,
        scratch_shapes=[pltpu.VMEM((64, R), F32)],
        name="downward",
    )(*args)


SUB = ("x", "c")
MORTON = ("g", "z")


def crossed(value, k):
    return lax.ppermute(value, SUB, [(i, i ^ k) for i in range(4)])


def local(multipoles, translations, upward_ops, downward_ops, targets_l6, source_boxes_level6, counts_l6,
          target_boxes_level5, anchors_l5, counts_l5, targets_l4, anchors_l4, counts_l4):
    q = lax.axis_index(SUB).astype(jnp.int32).reshape(1)
    peers = [crossed(multipoles, k) for k in (1, 2, 3)]
    spread, low6, hi6, low54, hi54, t54 = run_prep(
        q, multipoles, upward_ops, source_boxes_level6[0], counts_l6, anchors_l5[0], counts_l5, anchors_l4[0], counts_l4,
        target_boxes_level5[0], targets_l4[0])
    own = jnp.concatenate([multipoles] + peers, axis=0)
    n = lax.axis_size(MORTON)
    before = lax.ppermute(own, MORTON, [(i, i + 1) for i in range(n - 1)])
    after = lax.ppermute(own, MORTON, [(i + 1, i) for i in range(n - 1)])
    coarse = lax.all_to_all(spread, ("z",) + SUB, 0, 0)
    parts = run_main(q, own, before, after, coarse, translations, low6, hi6, low54, hi54, targets_l6[0], t54)
    received = [crossed(parts[k], k) for k in (1, 2, 3)]
    return run_final(parts[0], *received, downward_ops)


def solution(mesh):
    cut = Mesh(mesh.devices.reshape(8, 8, 2, 2), ("g", "z", "x", "c"))
    both = MORTON + SUB
    placed = (
        P(both, None),
        P(SUB, None, None),
        P(),
        P(),
        P(MORTON, SUB, None),
        P(MORTON, SUB, None),
        P(MORTON, SUB),
        P(MORTON, SUB, None),
        P(MORTON, SUB, None),
        P(MORTON, SUB),
        P(MORTON, SUB, None),
        P(MORTON, SUB, None),
        P(MORTON, SUB),
    )
    return jax.shard_map(local, mesh=cut, in_specs=placed, out_specs=P(both, None), check_vma=False)
```

```python
import jax
import jax.numpy as jnp
from jax import lax
from jax.experimental import pallas as pl
from jax.experimental.pallas import tpu as pltpu
from jax.sharding import Mesh
from jax.sharding import PartitionSpec as P

R = 128
NO = 79
G = 40
BF = jnp.bfloat16
F32 = jnp.float32


def iota(shape, dim):
    return lax.broadcasted_iota(jnp.int32, shape, dim)


def prep_kernel(q_ref, m_ref, up_ref, src_ref, c6_ref, a5_ref, c5_ref, a4_ref, c4_ref, t5_ref, t4_ref,
                grp_ref, low6_ref, hi6_ref, low54_ref, hi54_ref, t54_ref, sq_ref, st_ref):
    q = q_ref[0]
    st_ref[pl.ds(0, 64), :] = m_ref[...].astype(F32)
    c5 = jnp.zeros((8, R), F32)
    for c in range(8):
        rows = st_ref[pl.ds(c, 8, stride=8), :].astype(BF)
        c5 = c5 + jnp.dot(rows, up_ref[c], preferred_element_type=F32)
    c5r = c5.astype(BF).astype(F32)
    c4 = jnp.zeros((8, R), F32)
    for c in range(8):
        rows = jnp.broadcast_to(c5r[c : c + 1, :], (8, R)).astype(BF)
        c4 = c4 + jnp.dot(rows, up_ref[c], preferred_element_type=F32)
    both = jnp.concatenate([c5, c4], axis=0).astype(BF)
    grp_ref[...] = jnp.broadcast_to(both[None], (32, 16, R))

    sq_ref[...] = jnp.zeros((R, R), F32)
    sq_ref[0:NO, :] = src_ref[...].reshape(NO, R).astype(F32)
    src = sq_ref[...].T.astype(jnp.int32)

    def live(c_ref, rows):
        sq_ref[0:1, :] = jnp.zeros((1, R), F32)
        sq_ref[0:1, 0:NO] = c_ref[...].astype(F32)
        counts = jnp.broadcast_to(sq_ref[0:1, :], (rows, R))
        return iota((rows, R), 0).astype(F32) < counts

    low = jnp.bitwise_xor(jnp.bitwise_and(src, 255), q * 64)
    low6_ref[...] = jnp.where(live(c6_ref, R), low.astype(F32), -1.0)
    hi6_ref[...] = jnp.right_shift(src, 8).astype(F32)
    a5 = a5_ref[...]
    sq_ref[0:16, 0:NO] = (16 * jnp.right_shift(a5, 3) + jnp.bitwise_and(a5, 7)).astype(F32)
    code5 = sq_ref[0:16, :]
    code5 = jnp.where(live(c5_ref, 16), code5, -1.0)
    sq_ref[0:2, 0:NO] = (16 * a4_ref[...] + 8).astype(F32)
    code4 = sq_ref[0:16, :]
    code4 = jnp.where(live(c4_ref, 16), code4, -1.0)
    code = jnp.concatenate([code5, code4], axis=0)
    upper = code >= 256.0
    low54_ref[...] = jnp.where(upper, code - 256.0, code)
    hi54_ref[...] = upper.astype(F32)
    sq_ref[...] = jnp.full((R, R), -1.0, F32)
    sq_ref[0:16, 0:NO] = t5_ref[...].astype(F32)
    sq_ref[16:18, 0:NO] = t4_ref[...].astype(F32) + 32.0
    sq_ref[...] = sq_ref[...].T
    packed = sq_ref[pl.ds(0, 24, stride=4), :]
    lane = iota((24, R), 1)
    for i in range(1, 4):
        part = pltpu.roll(sq_ref[pl.ds(i, 24, stride=4), :], 32 * i, 1)
        packed = jnp.where(lane >= 32 * i, part, packed)
    t54_ref[...] = packed


def main_kernel(q_ref, own_ref, prev_ref, next_ref, grp_ref, t_ref, low6_ref, hi6_ref, low54_ref, hi54_ref,
                tgt_ref, t54_ref, o0_ref, o1_ref, o2_ref, o3_ref, x_ref, x54_ref, acc_ref, acc54_ref, tf_ref):
    x_ref[:, 0:R] = prev_ref[...]
    x_ref[:, R : 2 * R] = own_ref[...]
    x_ref[:, 2 * R : 3 * R] = next_ref[...]
    x54_ref[:, 0:R] = grp_ref[0:16].reshape(256, R)
    x54_ref[:, R : 2 * R] = grp_ref[16:32].reshape(256, R)
    acc_ref[...] = jnp.zeros_like(acc_ref)
    acc54_ref[...] = jnp.zeros_like(acc54_ref)
    tf_ref[0:NO, :] = tgt_ref[...].reshape(NO, R).astype(F32)

    def hot(column, rows):
        wide = jnp.broadcast_to(column, (rows, R)).astype(BF)
        lane = iota((rows, R), 1).astype(BF)
        one = jnp.ones((rows, R), BF)
        zero = jnp.zeros((rows, R), BF)
        left = jnp.where(wide == lane, one, zero)
        right = jnp.where(wide == lane + jnp.asarray(128, BF), one, zero)
        return jnp.concatenate([left, right], axis=1)

    def placing(row, rows, base):
        wide = jnp.broadcast_to(row, (rows, R)).astype(BF)
        down = (iota((rows, R), 0) + base).astype(BF)
        return jnp.where(wide == down, jnp.ones((rows, R), BF), jnp.zeros((rows, R), BF))

    def group(g, count):
        first = g * G
        shift = lax.rem(R - first, R)
        low6 = pltpu.roll(low6_ref[...], shift, 1)
        hi6 = pltpu.roll(hi6_ref[...], shift, 1)
        low54 = pltpu.roll(low54_ref[...], shift, 1)
        hi54 = pltpu.roll(hi54_ref[...], shift, 1)
        hots = jnp.concatenate([hot(low6[:, i : i + 1], R) for i in range(count)], axis=0)
        picked = jnp.dot(hots, x_ref[...], preferred_element_type=F32)
        hots = jnp.concatenate([hot(low54[:, i : i + 1], 32) for i in range(count)], axis=0)
        few = jnp.dot(hots, x54_ref[...], preferred_element_type=F32)
        ys, y54s, places = [], [], []
        for i in range(count):
            seg = jnp.broadcast_to(hi6[:, i : i + 1], (R, R))
            p = picked[i * R : (i + 1) * R]
            p = jnp.where(seg == 0.0, p[:, 0:R], jnp.where(seg == 1.0, p[:, R : 2 * R], p[:, 2 * R :]))
            seg = jnp.broadcast_to(hi54[:, i : i + 1], (32, R))
            w = few[i * 32 : (i + 1) * 32]
            w = jnp.where(seg == 0.0, w[:, 0:R], w[:, R:])
            rows = jnp.concatenate([p.astype(BF), w.astype(BF)], axis=0)
            y = jnp.dot(rows, t_ref[first + i], preferred_element_type=F32).astype(BF)
            ys.append(y[0:R])
            y54s.append(y[R:])
            places.append(placing(tf_ref[pl.ds(first + i, 1), :], 256, 0))
        acc_ref[...] += jnp.dot(jnp.concatenate(places, axis=1), jnp.concatenate(ys, axis=0), preferred_element_type=F32)
        if count % 4:
            y54s.append(jnp.zeros((32 * (4 - count % 4), R), BF))
        n = (count + 3) // 4
        p54 = jnp.concatenate([placing(t54_ref[pl.ds(g * (G // 4) + j, 1), :], 48, 0) for j in range(n)], axis=1)
        acc54_ref[...] += jnp.dot(p54, jnp.concatenate(y54s, axis=0), preferred_element_type=F32)

    def body(g, carry):
        group(g, G)
        return carry

    lax.fori_loop(0, NO // G, body, 0)
    group(NO // G, NO % G)
    q = q_ref[0]
    acc54_ref[0:32] = acc54_ref[0:32] * 0.5
    acc54_ref[32:48] = acc54_ref[32:48] * 0.25
    for k, out in enumerate((o0_ref, o1_ref, o2_ref, o3_ref)):
        d = jnp.bitwise_xor(q, k)
        out[0:64] = acc_ref[pl.ds(64 * d, 64), :].astype(BF)
        five = acc54_ref[pl.ds(8 * d, 8), :]
        four = jnp.broadcast_to(acc54_ref[pl.ds(32 + d, 1), :], (8, R))
        small = jnp.concatenate([five, four], axis=0)
        top = small.astype(BF)
        out[64:80] = top
        out[80:96] = (small - top.astype(F32)).astype(BF)


def final_kernel(a_ref, b_ref, c_ref, d_ref, dn_ref, out_ref, s_ref):
    total = (a_ref[...].astype(F32) + b_ref[...].astype(F32)) + (c_ref[...].astype(F32) + d_ref[...].astype(F32))
    small = total[64:80] + total[80:96]
    far5 = small[0:8]
    local4 = small[8:16].astype(BF)
    row = iota((8, R), 0)
    local5 = far5
    for c in range(8):
        spread = jnp.dot(local4, dn_ref[c], preferred_element_type=F32)
        local5 = local5 + jnp.where(row == c, spread, 0.0)
    local5 = local5.astype(BF)
    for c in range(8):
        s_ref[pl.ds(c, 8, stride=8), :] = jnp.dot(local5, dn_ref[c], preferred_element_type=F32)
    out_ref[...] = (total[0:64] + s_ref[...]).astype(BF)


VM = pl.BlockSpec(memory_space=pltpu.VMEM)
SM = pl.BlockSpec(memory_space=pltpu.SMEM)


def shape(dims, kind=F32):
    return jax.ShapeDtypeStruct(dims, kind)


def run_prep(q, *args):
    return pl.pallas_call(
        prep_kernel,
        out_shape=(shape((32, 16, R), BF), shape((R, R)), shape((R, R)), shape((32, R)), shape((32, R)), shape((24, R))),
        in_specs=[SM] + [VM] * len(args),
        out_specs=tuple([VM] * 6),
        scratch_shapes=[pltpu.VMEM((R, R), F32), pltpu.VMEM((64, R), F32)],
        name="prep",
    )(q, *args)


def run_main(q, *args):
    return pl.pallas_call(
        main_kernel,
        out_shape=tuple([shape((96, R), BF)] * 4),
        in_specs=[SM] + [VM] * len(args),
        out_specs=tuple([VM] * 4),
        scratch_shapes=[
            pltpu.VMEM((256, 3 * R), BF),
            pltpu.VMEM((256, 2 * R), BF),
            pltpu.VMEM((256, R), F32),
            pltpu.VMEM((48, R), F32),
            pltpu.VMEM((80, R), F32),
        ],
        name="translate",
    )(q, *args)


def run_final(*args):
    return pl.pallas_call(
        final_kernel,
        out_shape=shape((64, R), BF),
        in_specs=[VM] * len(args),
        out_specs=VM,
        scratch_shapes=[pltpu.VMEM((64, R), F32)],
        name="downward",
    )(*args)


SUB = ("x", "c")
MORTON = ("g", "z")


def rows_of(table):
    return table.transpose(1, 0, 2)


def crossed(value, k):
    return lax.ppermute(value, SUB, [(i, i ^ k) for i in range(4)])


def local(multipoles, translations, upward_ops, downward_ops, targets_l6, source_boxes_level6, counts_l6,
          target_boxes_level5, anchors_l5, counts_l5, targets_l4, anchors_l4, counts_l4):
    q = lax.axis_index(SUB).astype(jnp.int32).reshape(1)
    peers = [crossed(multipoles, k) for k in (1, 2, 3)]
    spread, low6, hi6, low54, hi54, t54 = run_prep(
        q, multipoles, upward_ops, rows_of(source_boxes_level6), counts_l6, anchors_l5[0].T, counts_l5, anchors_l4[0].T, counts_l4,
        target_boxes_level5[0].T, targets_l4[0].T)
    own = jnp.concatenate([multipoles] + peers, axis=0)
    n = lax.axis_size(MORTON)
    before = lax.ppermute(own, MORTON, [(i, i + 1) for i in range(n - 1)])
    after = lax.ppermute(own, MORTON, [(i + 1, i) for i in range(n - 1)])
    coarse = lax.all_to_all(spread, ("z",) + SUB, 0, 0)
    parts = run_main(q, own, before, after, coarse, translations, low6, hi6, low54, hi54, rows_of(targets_l6), t54)
    received = [crossed(parts[k], k) for k in (1, 2, 3)]
    return run_final(parts[0], *received, downward_ops)


def solution(mesh):
    cut = Mesh(mesh.devices.reshape(8, 8, 2, 2), ("g", "z", "x", "c"))
    both = MORTON + SUB
    placed = (
        P(both, None),
        P(SUB, None, None),
        P(),
        P(),
        P(MORTON, SUB, None),
        P(MORTON, SUB, None),
        P(MORTON, SUB),
        P(MORTON, SUB, None),
        P(MORTON, SUB, None),
        P(MORTON, SUB),
        P(MORTON, SUB, None),
        P(MORTON, SUB, None),
        P(MORTON, SUB),
    )
    return jax.shard_map(local, mesh=cut, in_specs=placed, out_specs=P(both, None), check_vma=False)
```

```python
import jax
import jax.numpy as jnp
from jax import lax
from jax.experimental import pallas as pl
from jax.experimental.pallas import tpu as pltpu
from jax.sharding import Mesh
from jax.sharding import PartitionSpec as P


R = 128
NO = 79
G = 20
HELD = 20
BF = jnp.bfloat16
F32 = jnp.float32


def iota(shape, dim):
    return lax.broadcasted_iota(jnp.int32, shape, dim)


def prep_kernel(q_ref, m_ref, up_ref, src_ref, c6_ref, a5_ref, c5_ref, a4_ref, c4_ref, t5_ref, t4_ref, t6_ref, t_hbm,
                grp_ref, low6_ref, hi6_ref, low54_ref, hi54_ref, t54_ref, tgt_ref, own_ref, t_ref, sq_ref, st_ref, sem):
    fetch = pltpu.make_async_copy(t_hbm.at[pl.ds(0, HELD)], t_ref, sem)
    fetch.start()
    own_ref[0:64] = m_ref[...]
    own_ref[64:256] = jnp.zeros((192, R), BF)
    tgt_ref[0:NO, :] = t6_ref[...].reshape(NO, R).astype(F32)
    tgt_ref[NO:80, :] = jnp.zeros((80 - NO, R), F32)
    q = q_ref[0]
    st_ref[pl.ds(0, 64), :] = m_ref[...].astype(F32)
    c5 = jnp.zeros((8, R), F32)
    for c in range(8):
        rows = st_ref[pl.ds(c, 8, stride=8), :].astype(BF)
        c5 = c5 + jnp.dot(rows, up_ref[c], preferred_element_type=F32)
    c5r = c5.astype(BF).astype(F32)
    c4 = jnp.zeros((8, R), F32)
    for c in range(8):
        rows = jnp.broadcast_to(c5r[c : c + 1, :], (8, R)).astype(BF)
        c4 = c4 + jnp.dot(rows, up_ref[c], preferred_element_type=F32)
    both = jnp.concatenate([c5, c4], axis=0).astype(BF)
    grp_ref[...] = jnp.broadcast_to(both[None], (32, 16, R))

    sq_ref[...] = jnp.zeros((R, R), F32)
    sq_ref[0:NO, :] = src_ref[...].reshape(NO, R).astype(F32)
    src = sq_ref[...].T.astype(jnp.int32)

    def live(c_ref, rows):
        sq_ref[0:1, :] = jnp.zeros((1, R), F32)
        sq_ref[0:1, 0:NO] = c_ref[...].astype(F32)
        counts = jnp.broadcast_to(sq_ref[0:1, :], (rows, R))
        return iota((rows, R), 0).astype(F32) < counts

    low = jnp.bitwise_xor(jnp.bitwise_and(src, 255), q * 64)
    low6_ref[...] = jnp.where(live(c6_ref, R), low.astype(F32), -1.0).astype(BF)
    hi6_ref[...] = jnp.right_shift(src, 8).astype(F32).astype(BF)
    a5 = a5_ref[...]
    sq_ref[0:16, 0:NO] = (16 * jnp.right_shift(a5, 3) + jnp.bitwise_and(a5, 7)).astype(F32)
    code5 = sq_ref[0:16, :]
    code5 = jnp.where(live(c5_ref, 16), code5, -1.0)
    sq_ref[0:2, 0:NO] = (16 * a4_ref[...] + 8).astype(F32)
    code4 = sq_ref[0:16, :]
    code4 = jnp.where(live(c4_ref, 16), code4, -1.0)
    code = jnp.concatenate([code5, code4], axis=0)
    upper = code >= 256.0
    low54_ref[...] = jnp.where(upper, code - 256.0, code).astype(BF)
    hi54_ref[...] = upper.astype(F32).astype(BF)
    sq_ref[...] = jnp.full((R, R), -1.0, F32)
    sq_ref[0:16, 0:NO] = t5_ref[...].astype(F32)
    sq_ref[16:18, 0:NO] = t4_ref[...].astype(F32) + 32.0
    sq_ref[...] = sq_ref[...].T
    packed = sq_ref[pl.ds(0, 24, stride=4), :]
    lane = iota((24, R), 1)
    for i in range(1, 4):
        part = pltpu.roll(sq_ref[pl.ds(i, 24, stride=4), :], 32 * i, 1)
        packed = jnp.where(lane >= 32 * i, part, packed)
    t54_ref[...] = packed
    fetch.wait()


def hot(column, rows):
    wide = jnp.broadcast_to(column, (rows, R))
    lane = iota((rows, R), 1)
    one = jnp.ones((rows, R), BF)
    zero = jnp.zeros((rows, R), BF)
    left = jnp.where(wide == lane.astype(BF), one, zero)
    right = jnp.where(wide == (lane + R).astype(BF), one, zero)
    return jnp.concatenate([left, right], axis=1)


def placing(row, rows):
    wide = jnp.broadcast_to(row, (rows, R)).astype(BF)
    down = iota((rows, R), 0).astype(BF)
    return jnp.where(wide == down, jnp.ones((rows, R), BF), jnp.zeros((rows, R), BF))


def fine_kernel(z_ref, g_ref, own_ref, prev_ref, next_ref, far_ref, h_ref, low_ref, hi_ref, tgt_ref, t_hbm, acc_ref, t_ref, x_ref, sem):
    fetch = pltpu.make_async_copy(t_hbm.at[pl.ds(HELD, NO - HELD)], t_ref, sem)
    fetch.start()
    z = z_ref[0]
    x_ref[:, R : 2 * R] = own_ref[...]

    g = g_ref[0]
    nothing = jnp.zeros((256, R), BF)

    @pl.when(z == 0)
    def _():
        x_ref[:, 0:R] = jnp.where(g > 0, far_ref[...], nothing)

    @pl.when(z > 0)
    def _():
        x_ref[:, 0:R] = prev_ref[...]

    @pl.when(z == 7)
    def _():
        x_ref[:, 2 * R : 3 * R] = jnp.where(g < 7, far_ref[...], nothing)

    @pl.when(z < 7)
    def _():
        x_ref[:, 2 * R : 3 * R] = next_ref[...]

    low = low_ref[...]
    hi = hi_ref[...]
    for first in range(0, NO, G):
        ops = range(first, min(first + G, NO))
        hots = jnp.concatenate([hot(low[:, o : o + 1], R) for o in ops], axis=0)
        found = jnp.dot(hots, x_ref[...], preferred_element_type=F32).astype(BF)
        if first == HELD:
            fetch.wait()
        ys, places = [], []
        for n, o in enumerate(ops):
            seg = jnp.broadcast_to(hi[:, o : o + 1], (R, R))
            p = found[n * R : (n + 1) * R]
            p = jnp.where(seg == jnp.asarray(0, BF), p[:, 0:R], jnp.where(seg == jnp.asarray(1, BF), p[:, R : 2 * R], p[:, 2 * R :]))
            operator = h_ref[o] if o < HELD else t_ref[o - HELD]
            ys.append(jnp.dot(p, operator, preferred_element_type=F32).astype(BF))
            places.append(placing(tgt_ref[o : o + 1, :], 256))
        added = jnp.dot(jnp.concatenate(places, axis=1), jnp.concatenate(ys, axis=0), preferred_element_type=F32)
        if first == 0:
            acc_ref[...] = added
        else:
            acc_ref[...] += added


def coarse_kernel(q_ref, acc_ref, grp_ref, h_ref, t_ref, low_ref, hi_ref, t54_ref, o0_ref, o1_ref, o2_ref, o3_ref, x_ref, far_ref):
    x_ref[:, 0:R] = grp_ref[0:16].reshape(256, R)
    x_ref[:, R : 2 * R] = grp_ref[16:32].reshape(256, R)
    low = low_ref[...]
    hi = hi_ref[...]
    for first in range(0, NO, G):
        ops = range(first, min(first + G, NO))
        hots = jnp.concatenate([hot(low[:, o : o + 1], 32) for o in ops], axis=0)
        found = jnp.dot(hots, x_ref[...], preferred_element_type=F32).astype(BF)
        ys = []
        for n, o in enumerate(ops):
            seg = jnp.broadcast_to(hi[:, o : o + 1], (32, R))
            p = found[n * 32 : (n + 1) * 32]
            p = jnp.where(seg == jnp.asarray(0, BF), p[:, 0:R], p[:, R:])
            operator = h_ref[o] if o < HELD else t_ref[o - HELD]
            ys.append(jnp.dot(p, operator, preferred_element_type=F32).astype(BF))
        short = -len(ops) % 4
        if short:
            ys.append(jnp.zeros((32 * short, R), BF))
        rows = range(first // 4, (first + len(ops) + 3) // 4)
        places = jnp.concatenate([placing(t54_ref[j : j + 1, :], 48) for j in rows], axis=1)
        added = jnp.dot(places, jnp.concatenate(ys, axis=0), preferred_element_type=F32)
        if first == 0:
            far_ref[...] = added
        else:
            far_ref[...] += added
    q = q_ref[0]
    far_ref[0:32] = far_ref[0:32] * 0.5
    far_ref[32:48] = far_ref[32:48] * 0.25
    for k, out in enumerate((o0_ref, o1_ref, o2_ref, o3_ref)):
        d = jnp.bitwise_xor(q, k)
        out[0:64] = acc_ref[pl.ds(64 * d, 64), :].astype(BF)
        five = far_ref[pl.ds(8 * d, 8), :]
        four = jnp.broadcast_to(far_ref[pl.ds(32 + d, 1), :], (8, R))
        small = jnp.concatenate([five, four], axis=0)
        top = small.astype(BF)
        out[64:80] = top
        out[80:96] = (small - top.astype(F32)).astype(BF)


def final_kernel(a_ref, b_ref, c_ref, d_ref, dn_ref, out_ref, s_ref):
    total = (a_ref[...].astype(F32) + b_ref[...].astype(F32)) + (c_ref[...].astype(F32) + d_ref[...].astype(F32))
    small = total[64:80] + total[80:96]
    far5 = small[0:8]
    local4 = small[8:16].astype(BF)
    row = iota((8, R), 0)
    local5 = far5
    for c in range(8):
        spread = jnp.dot(local4, dn_ref[c], preferred_element_type=F32)
        local5 = local5 + jnp.where(row == c, spread, 0.0)
    local5 = local5.astype(BF)
    for c in range(8):
        s_ref[pl.ds(c, 8, stride=8), :] = jnp.dot(local5, dn_ref[c], preferred_element_type=F32)
    out_ref[...] = (total[0:64] + s_ref[...]).astype(BF)


VM = pl.BlockSpec(memory_space=pltpu.VMEM)
SM = pl.BlockSpec(memory_space=pltpu.SMEM)
FAR = pl.BlockSpec(memory_space=pl.ANY)
LIMIT = pltpu.CompilerParams(vmem_limit_bytes=24 * 1024 * 1024)


def near_core(value):
    return pltpu.with_memory_space_constraint(value, pltpu.VMEM)


def in_hbm(value):
    return pltpu.with_memory_space_constraint(value, pltpu.HBM)


def call(kernel, outs, scratch, vectors, scalars=(), far=0):
    return pl.pallas_call(
        kernel,
        out_shape=tuple(pltpu.VMEM(dims, kind) for dims, kind in outs),
        in_specs=[SM] * len(scalars) + [VM] * (len(vectors) - far) + [FAR] * far,
        out_specs=tuple([VM] * len(outs)),
        scratch_shapes=scratch,
        compiler_params=LIMIT,
    )(*scalars, *vectors)


SUB = ("x", "c")
MORTON = ("g", "z")


def rows_of(table):
    return table.transpose(1, 0, 2)


def crossed(value, k):
    return lax.ppermute(value, SUB, [(i, i ^ k) for i in range(4)])


def local(multipoles, translations, upward_ops, downward_ops, targets_l6, source_boxes_level6, counts_l6,
          target_boxes_level5, anchors_l5, counts_l5, targets_l4, anchors_l4, counts_l4):
    q = lax.axis_index(SUB).astype(jnp.int32).reshape(1)
    z = lax.axis_index("z").astype(jnp.int32).reshape(1)
    g = lax.axis_index("g").astype(jnp.int32).reshape(1)
    groups, ring = lax.axis_size("g"), lax.axis_size("z")
    peers = [crossed(multipoles, k) for k in (1, 2, 3)]
    spread, low6, hi6, low54, hi54, t54, tgt, own, held = call(
        prep_kernel,
        [((32, 16, R), BF), ((R, R), BF), ((R, R), BF), ((32, R), BF), ((32, R), BF), ((24, R), F32), ((80, R), F32),
         ((256, R), BF), ((HELD, R, R), BF)],
        [pltpu.VMEM((R, R), F32), pltpu.VMEM((64, R), F32), pltpu.SemaphoreType.DMA],
        [*map(in_hbm, (multipoles, upward_ops, rows_of(source_boxes_level6), counts_l6, anchors_l5[0].T, counts_l5,
                       anchors_l4[0].T, counts_l4, target_boxes_level5[0].T, targets_l4[0].T, rows_of(targets_l6), translations))],
        [q], far=1)
    for k, peer in enumerate(peers):
        own = lax.dynamic_update_slice(own, peer, (64 * k + 64, 0))
    before = lax.ppermute(own, "z", [(i, (i + 1) % ring) for i in range(ring)])
    after = lax.ppermute(own, "z", [((i + 1) % ring, i) for i in range(ring)])
    ends = [(i * ring + ring - 1, i * ring + ring) for i in range(groups - 1)]
    ends = dict(ends + [(j, i) for i, j in ends])
    far = lax.ppermute(own, MORTON, [(i, ends.get(i, i)) for i in range(groups * ring)])
    coarse = lax.all_to_all(spread, ("z",) + SUB, 0, 0)
    fine, rest = call(fine_kernel, [((256, R), F32), ((NO - HELD, R, R), BF)],
                   [pltpu.VMEM((256, 3 * R), BF), pltpu.SemaphoreType.DMA],
                   [*map(near_core, (own, before, after, far, held, low6, hi6, tgt)), in_hbm(translations)], [z, g], far=1)
    parts = call(coarse_kernel, [((96, R), BF)] * 4, [pltpu.VMEM((256, 2 * R), BF), pltpu.VMEM((48, R), F32)],
                 [*map(near_core, (fine, coarse, held, rest, low54, hi54, t54))], [q])
    received = [crossed(parts[k], k) for k in (1, 2, 3)]
    return pl.pallas_call(
        final_kernel,
        out_shape=jax.ShapeDtypeStruct((64, R), BF),
        in_specs=[VM] * 5,
        out_specs=VM,
        scratch_shapes=[pltpu.VMEM((64, R), F32)],
        compiler_params=LIMIT,
        name="downward",
    )(*[near_core(v) for v in (parts[0], *received, downward_ops)])


def solution(mesh):
    cut = Mesh(mesh.devices.reshape(8, 8, 2, 2), ("g", "z", "x", "c"))
    both = MORTON + SUB
    placed = (
        P(both, None),
        P(SUB, None, None),
        P(),
        P(),
        P(MORTON, SUB, None),
        P(MORTON, SUB, None),
        P(MORTON, SUB),
        P(MORTON, SUB, None),
        P(MORTON, SUB, None),
        P(MORTON, SUB),
        P(MORTON, SUB, None),
        P(MORTON, SUB, None),
        P(MORTON, SUB),
    )
    return jax.shard_map(local, mesh=cut, in_specs=placed, out_specs=P(both, None), check_vma=False)
```

```python
import jax
import jax.numpy as jnp
from jax import lax
from jax.experimental import pallas as pl
from jax.experimental.pallas import tpu as pltpu
from jax.sharding import Mesh
from jax.sharding import PartitionSpec as P


R = 128
NO = 79
G = 20
BF = jnp.bfloat16
F32 = jnp.float32


def iota(shape, dim):
    return lax.broadcasted_iota(jnp.int32, shape, dim)


def upward_kernel(m_ref, up_ref, pack_ref, st_ref):
    st_ref[...] = m_ref[...].astype(F32)
    c5 = jnp.zeros((8, R), F32)
    for c in range(8):
        rows = st_ref[pl.ds(c, 8, stride=8), :].astype(BF)
        c5 = c5 + jnp.dot(rows, up_ref[c], preferred_element_type=F32)
    c5r = c5.astype(BF).astype(F32)
    c4 = jnp.zeros((8, R), F32)
    for c in range(8):
        rows = jnp.broadcast_to(c5r[c : c + 1, :], (8, R)).astype(BF)
        c4 = c4 + jnp.dot(rows, up_ref[c], preferred_element_type=F32)
    pack_ref[0:64] = m_ref[...]
    pack_ref[64:80] = jnp.concatenate([c5, c4], axis=0).astype(BF)


def prep_kernel(i_ref, pack_ref, src_hbm, c6_hbm, a5_hbm, c5_hbm, a4_hbm, c4_hbm, t5_hbm, t4_hbm, t6_hbm, t_hbm,
                low6_ref, hi6_ref, low54_ref, hi54_ref, t54_ref, tgt_ref, own_ref, r0_ref, t_ref, sq_ref,
                src_ref, c6_ref, a5_ref, c5_ref, a4_ref, c4_ref, t5_ref, t4_ref, t6_ref, sems):
    pairs = ((src_hbm, src_ref), (c6_hbm, c6_ref), (a5_hbm, a5_ref), (c5_hbm, c5_ref),
             (a4_hbm, a4_ref), (c4_hbm, c4_ref), (t5_hbm, t5_ref), (t4_hbm, t4_ref), (t6_hbm, t6_ref), (t_hbm, t_ref))
    fetches = [pltpu.make_async_copy(source, place, sems.at[i]) for i, (source, place) in enumerate(pairs)]
    for fetch in fetches:
        fetch.start()
    own_ref[0:64] = pack_ref[0:64]
    own_ref[64:256] = jnp.zeros((192, R), BF)
    r0_ref[0:16] = pack_ref[64:80]
    r0_ref[16:64] = jnp.zeros((48, R), BF)
    for fetch in fetches[:-1]:
        fetch.wait()
    i = i_ref[0]
    q = jnp.bitwise_and(i, 3)
    tgt_ref[0:NO, :] = t6_ref[...].reshape(NO, R).astype(F32)
    tgt_ref[NO:80, :] = jnp.zeros((80 - NO, R), F32)

    sq_ref[...] = jnp.zeros((R, R), F32)
    sq_ref[0:NO, :] = src_ref[...].reshape(NO, R).astype(F32)
    src = sq_ref[...].T.astype(jnp.int32)

    def live(c_ref, rows):
        sq_ref[0:1, :] = jnp.zeros((1, R), F32)
        sq_ref[0:1, 0:NO] = c_ref[...].astype(F32)
        counts = jnp.broadcast_to(sq_ref[0:1, :], (rows, R))
        return iota((rows, R), 0).astype(F32) < counts

    low = jnp.bitwise_xor(jnp.bitwise_and(src, 255), q * 64)
    low6_ref[...] = jnp.where(live(c6_ref, R), low.astype(F32), -1.0).astype(BF)
    hi6_ref[...] = jnp.right_shift(src, 8).astype(F32).astype(BF)
    a5 = a5_ref[...]
    sq_ref[0:16, 0:NO] = (16 * jnp.bitwise_xor(jnp.right_shift(a5, 3), i) + jnp.bitwise_and(a5, 7)).astype(F32)
    code5 = sq_ref[0:16, :]
    code5 = jnp.where(live(c5_ref, 16), code5, -1.0)
    sq_ref[0:2, 0:NO] = (16 * jnp.bitwise_xor(a4_ref[...], i) + 8).astype(F32)
    code4 = sq_ref[0:16, :]
    code4 = jnp.where(live(c4_ref, 16), code4, -1.0)
    code = jnp.concatenate([code5, code4], axis=0)
    upper = code >= 256.0
    low54_ref[...] = jnp.where(upper, code - 256.0, code).astype(BF)
    hi54_ref[...] = upper.astype(F32).astype(BF)
    sq_ref[...] = jnp.full((R, R), -1.0, F32)
    sq_ref[0:16, 0:NO] = t5_ref[...].astype(F32)
    sq_ref[16:18, 0:NO] = t4_ref[...].astype(F32) + 32.0
    sq_ref[...] = sq_ref[...].T
    packed = sq_ref[pl.ds(0, 24, stride=4), :]
    lane = iota((24, R), 1)
    for i in range(1, 4):
        part = pltpu.roll(sq_ref[pl.ds(i, 24, stride=4), :], 32 * i, 1)
        packed = jnp.where(lane >= 32 * i, part, packed)
    t54_ref[...] = packed
    fetches[-1].wait()


def hot(column, rows):
    wide = jnp.broadcast_to(column, (rows, R))
    lane = iota((rows, R), 1)
    one = jnp.ones((rows, R), BF)
    zero = jnp.zeros((rows, R), BF)
    left = jnp.where(wide == lane.astype(BF), one, zero)
    right = jnp.where(wide == (lane + R).astype(BF), one, zero)
    return jnp.concatenate([left, right], axis=1)


def placing(row, rows):
    wide = jnp.broadcast_to(row, (rows, R)).astype(BF)
    down = iota((rows, R), 0).astype(BF)
    return jnp.where(wide == down, jnp.ones((rows, R), BF), jnp.zeros((rows, R), BF))


def fine_kernel(z_ref, g_ref, own_ref, prev_ref, next_ref, far_ref, t_ref, low_ref, hi_ref, tgt_ref, acc_ref, x_ref):
    z = z_ref[0]
    x_ref[:, R : 2 * R] = own_ref[...]

    g = g_ref[0]
    nothing = jnp.zeros((256, R), BF)

    @pl.when(z == 0)
    def _():
        x_ref[:, 0:R] = jnp.where(g > 0, far_ref[...], nothing)

    @pl.when(z > 0)
    def _():
        x_ref[:, 0:R] = prev_ref[...]

    @pl.when(z == 7)
    def _():
        x_ref[:, 2 * R : 3 * R] = jnp.where(g < 7, far_ref[...], nothing)

    @pl.when(z < 7)
    def _():
        x_ref[:, 2 * R : 3 * R] = next_ref[...]

    low = low_ref[...]
    hi = hi_ref[...]
    for first in range(0, NO, G):
        ops = range(first, min(first + G, NO))
        hots = jnp.concatenate([hot(low[:, o : o + 1], R) for o in ops], axis=0)
        found = jnp.dot(hots, x_ref[...], preferred_element_type=F32).astype(BF)
        ys, places = [], []
        for n, o in enumerate(ops):
            seg = jnp.broadcast_to(hi[:, o : o + 1], (R, R))
            p = found[n * R : (n + 1) * R]
            p = jnp.where(seg == jnp.asarray(0, BF), p[:, 0:R], jnp.where(seg == jnp.asarray(1, BF), p[:, R : 2 * R], p[:, 2 * R :]))
            ys.append(jnp.dot(p, t_ref[o], preferred_element_type=F32).astype(BF))
            places.append(placing(tgt_ref[o : o + 1, :], 256))
        added = jnp.dot(jnp.concatenate(places, axis=1), jnp.concatenate(ys, axis=0), preferred_element_type=F32)
        if first == 0:
            acc_ref[...] = added
        else:
            acc_ref[...] += added


def coarse_kernel(q_ref, acc_ref, r0_ref, r1_ref, r2_ref, r3_ref, t_ref, low_ref, hi_ref, t54_ref,
                  o0_ref, o1_ref, o2_ref, o3_ref, x_ref, far_ref):
    x_ref[0:64, 0:R] = r0_ref[...]
    x_ref[64:128, 0:R] = r1_ref[...]
    x_ref[128:256, 0:R] = r2_ref[...]
    x_ref[:, R : 2 * R] = r3_ref[...]
    low = low_ref[...]
    hi = hi_ref[...]
    for first in range(0, NO, G):
        ops = range(first, min(first + G, NO))
        hots = jnp.concatenate([hot(low[:, o : o + 1], 32) for o in ops], axis=0)
        found = jnp.dot(hots, x_ref[...], preferred_element_type=F32).astype(BF)
        ys = []
        for n, o in enumerate(ops):
            seg = jnp.broadcast_to(hi[:, o : o + 1], (32, R))
            p = found[n * 32 : (n + 1) * 32]
            p = jnp.where(seg == jnp.asarray(0, BF), p[:, 0:R], p[:, R:])
            ys.append(jnp.dot(p, t_ref[o], preferred_element_type=F32).astype(BF))
        short = -len(ops) % 4
        if short:
            ys.append(jnp.zeros((32 * short, R), BF))
        rows = range(first // 4, (first + len(ops) + 3) // 4)
        places = jnp.concatenate([placing(t54_ref[j : j + 1, :], 48) for j in rows], axis=1)
        added = jnp.dot(places, jnp.concatenate(ys, axis=0), preferred_element_type=F32)
        if first == 0:
            far_ref[...] = added
        else:
            far_ref[...] += added
    q = q_ref[0]
    far_ref[0:32] = far_ref[0:32] * 0.5
    far_ref[32:48] = far_ref[32:48] * 0.25
    for k, out in enumerate((o0_ref, o1_ref, o2_ref, o3_ref)):
        d = jnp.bitwise_xor(q, k)
        out[0:64] = acc_ref[pl.ds(64 * d, 64), :].astype(BF)
        five = far_ref[pl.ds(8 * d, 8), :]
        four = jnp.broadcast_to(far_ref[pl.ds(32 + d, 1), :], (8, R))
        small = jnp.concatenate([five, four], axis=0)
        top = small.astype(BF)
        out[64:80] = top
        out[80:96] = (small - top.astype(F32)).astype(BF)


def final_kernel(a_ref, b_ref, c_ref, d_ref, dn_ref, out_ref, s_ref):
    total = (a_ref[...].astype(F32) + b_ref[...].astype(F32)) + (c_ref[...].astype(F32) + d_ref[...].astype(F32))
    small = total[64:80] + total[80:96]
    far5 = small[0:8]
    local4 = small[8:16].astype(BF)
    row = iota((8, R), 0)
    local5 = far5
    for c in range(8):
        spread = jnp.dot(local4, dn_ref[c], preferred_element_type=F32)
        local5 = local5 + jnp.where(row == c, spread, 0.0)
    local5 = local5.astype(BF)
    for c in range(8):
        s_ref[pl.ds(c, 8, stride=8), :] = jnp.dot(local5, dn_ref[c], preferred_element_type=F32)
    out_ref[...] = (total[0:64] + s_ref[...]).astype(BF)


VM = pl.BlockSpec(memory_space=pltpu.VMEM)
SM = pl.BlockSpec(memory_space=pltpu.SMEM)
FAR = pl.BlockSpec(memory_space=pl.ANY)
LIMIT = pltpu.CompilerParams(vmem_limit_bytes=24 * 1024 * 1024)


def near_core(value):
    return pltpu.with_memory_space_constraint(value, pltpu.VMEM)


def in_hbm(value):
    return pltpu.with_memory_space_constraint(value, pltpu.HBM)


def call(kernel, outs, scratch, vectors, scalars=(), far=0):
    return pl.pallas_call(
        kernel,
        out_shape=tuple(pltpu.VMEM(dims, kind) for dims, kind in outs),
        in_specs=[SM] * len(scalars) + [VM] * (len(vectors) - far) + [FAR] * far,
        out_specs=tuple([VM] * len(outs)),
        scratch_shapes=scratch,
        compiler_params=LIMIT,
    )(*scalars, *vectors)


SUB = ("x", "c")
MORTON = ("g", "z")


def rows_of(table):
    return table.transpose(1, 0, 2)


def crossed(value, k):
    return lax.ppermute(value, SUB, [(i, i ^ k) for i in range(4)])


def local(multipoles, translations, upward_ops, downward_ops, targets_l6, source_boxes_level6, counts_l6,
          target_boxes_level5, anchors_l5, counts_l5, targets_l4, anchors_l4, counts_l4):
    q = lax.axis_index(SUB).astype(jnp.int32).reshape(1)
    z = lax.axis_index("z").astype(jnp.int32).reshape(1)
    g = lax.axis_index("g").astype(jnp.int32).reshape(1)
    groups, ring = lax.axis_size("g"), lax.axis_size("z")
    ends = [(i * ring + ring - 1, i * ring + ring) for i in range(groups - 1)]
    ends = dict(ends + [(j, i) for i, j in ends])

    def doubled(value, bit):
        return lax.ppermute(value, "z", [(i, i ^ bit) for i in range(ring)])

    (pack,) = call(upward_kernel, [((80, R), BF)], [pltpu.VMEM((64, R), F32)], [in_hbm(multipoles), in_hbm(upward_ops)])
    peers = [crossed(pack, k) for k in (1, 2, 3)]
    low6, hi6, low54, hi54, t54, tgt, own, r0, held = call(
        prep_kernel,
        [((R, R), BF), ((R, R), BF), ((32, R), BF), ((32, R), BF), ((24, R), F32), ((80, R), F32),
         ((256, R), BF), ((64, R), BF), ((NO, R, R), BF)],
        [pltpu.VMEM((R, R), F32),
         pltpu.VMEM((NO, 1, R), jnp.int32), pltpu.VMEM((1, NO), jnp.int32), pltpu.VMEM((16, NO), jnp.int32),
         pltpu.VMEM((1, NO), jnp.int32), pltpu.VMEM((2, NO), jnp.int32), pltpu.VMEM((1, NO), jnp.int32),
         pltpu.VMEM((16, NO), jnp.int32), pltpu.VMEM((2, NO), jnp.int32), pltpu.VMEM((NO, 1, R), jnp.int32),
         pltpu.SemaphoreType.DMA((10,))],
        [near_core(pack), *map(in_hbm, (rows_of(source_boxes_level6), counts_l6, anchors_l5[0].T, counts_l5,
                       anchors_l4[0].T, counts_l4, target_boxes_level5[0].T, targets_l4[0].T, rows_of(targets_l6), translations))],
        [4 * z + q], far=10)
    for k, peer in enumerate(peers):
        own = lax.dynamic_update_slice(own, peer[0:64], (64 * k + 64, 0))
        r0 = lax.dynamic_update_slice(r0, peer[64:80], (16 * k + 16, 0))
    r1 = doubled(r0, 1)
    far = lax.ppermute(own, MORTON, [(i, ends.get(i, i)) for i in range(groups * ring)])
    r01 = jnp.concatenate([r0, r1], axis=0)
    r2 = doubled(r01, 2)
    before = lax.ppermute(own, "z", [(i, (i + 1) % ring) for i in range(ring)])
    after = lax.ppermute(own, "z", [((i + 1) % ring, i) for i in range(ring)])
    r02 = jnp.concatenate([r01, r2], axis=0)
    r3 = doubled(r02, 4)
    (fine,) = call(fine_kernel, [((256, R), F32)], [pltpu.VMEM((256, 3 * R), BF)],
                   [*map(near_core, (own, before, after, far, held, low6, hi6, tgt))], [z, g])
    parts = call(coarse_kernel, [((96, R), BF)] * 4, [pltpu.VMEM((256, 2 * R), BF), pltpu.VMEM((48, R), F32)],
                 [*map(near_core, (fine, r0, r1, r2, r3, held, low54, hi54, t54))], [q])
    received = [crossed(parts[k], k) for k in (1, 2, 3)]
    return pl.pallas_call(
        final_kernel,
        out_shape=jax.ShapeDtypeStruct((64, R), BF),
        in_specs=[VM] * 5,
        out_specs=VM,
        scratch_shapes=[pltpu.VMEM((64, R), F32)],
        compiler_params=LIMIT,
        name="downward",
    )(*[near_core(v) for v in (parts[0], *received, downward_ops)])


def solution(mesh):
    cut = Mesh(mesh.devices.reshape(8, 8, 2, 2), ("g", "z", "x", "c"))
    both = MORTON + SUB
    placed = (
        P(both, None),
        P(SUB, None, None),
        P(),
        P(),
        P(MORTON, SUB, None),
        P(MORTON, SUB, None),
        P(MORTON, SUB),
        P(MORTON, SUB, None),
        P(MORTON, SUB, None),
        P(MORTON, SUB),
        P(MORTON, SUB, None),
        P(MORTON, SUB, None),
        P(MORTON, SUB),
    )
    return jax.shard_map(local, mesh=cut, in_specs=placed, out_specs=P(both, None), check_vma=False)
```

```python
import jax
import jax.numpy as jnp
from jax import lax
from jax.experimental import pallas as pl
from jax.experimental.pallas import tpu as pltpu
from jax.sharding import Mesh
from jax.sharding import PartitionSpec as P


R = 128
NO = 79
G = 20
BF = jnp.bfloat16
F32 = jnp.float32


def iota(shape, dim):
    return lax.broadcasted_iota(jnp.int32, shape, dim)


def upward_kernel(m_ref, up_ref, pack_ref, st_ref):
    st_ref[...] = m_ref[...].astype(F32)
    c5 = jnp.zeros((8, R), F32)
    for c in range(8):
        rows = st_ref[pl.ds(c, 8, stride=8), :].astype(BF)
        c5 = c5 + jnp.dot(rows, up_ref[c], preferred_element_type=F32)
    c5r = c5.astype(BF).astype(F32)
    c4 = jnp.zeros((8, R), F32)
    for c in range(8):
        rows = jnp.broadcast_to(c5r[c : c + 1, :], (8, R)).astype(BF)
        c4 = c4 + jnp.dot(rows, up_ref[c], preferred_element_type=F32)
    pack_ref[0:64] = m_ref[...]
    pack_ref[64:80] = jnp.concatenate([c5, c4], axis=0).astype(BF)


def prep_kernel(i_ref, pack_ref, src_hbm, c6_hbm, a5_hbm, c5_hbm, a4_hbm, c4_hbm, t5_hbm, t4_hbm, t6_hbm, t_hbm,
                low6_ref, hi6_ref, low54_ref, hi54_ref, t54_ref, tgt_ref, own_ref, t_ref, sq_ref,
                src_ref, c6_ref, a5_ref, c5_ref, a4_ref, c4_ref, t5_ref, t4_ref, t6_ref, sems):
    pairs = ((src_hbm, src_ref), (c6_hbm, c6_ref), (a5_hbm, a5_ref), (c5_hbm, c5_ref),
             (a4_hbm, a4_ref), (c4_hbm, c4_ref), (t5_hbm, t5_ref), (t4_hbm, t4_ref), (t6_hbm, t6_ref), (t_hbm, t_ref))
    fetches = [pltpu.make_async_copy(source, place, sems.at[i]) for i, (source, place) in enumerate(pairs)]
    for fetch in fetches:
        fetch.start()
    own_ref[0:64] = pack_ref[0:64]
    own_ref[64:256] = jnp.zeros((192, R), BF)
    own_ref[256:272] = pack_ref[64:80]
    own_ref[272:320] = jnp.zeros((48, R), BF)
    for fetch in fetches[:-1]:
        fetch.wait()
    i = i_ref[0]
    q = jnp.bitwise_and(i, 3)
    z = jnp.right_shift(i, 2)

    def block(d):
        ahead = jnp.bitwise_and(jnp.right_shift(d, 2) - z, 7)
        return 64 * ahead + 16 * jnp.bitwise_xor(jnp.bitwise_and(d, 3), q)

    tgt_ref[0:NO, :] = t6_ref[...].reshape(NO, R).astype(F32)
    tgt_ref[NO:80, :] = jnp.zeros((80 - NO, R), F32)

    sq_ref[...] = jnp.zeros((R, R), F32)
    sq_ref[0:NO, :] = src_ref[...].reshape(NO, R).astype(F32)
    src = sq_ref[...].T.astype(jnp.int32)

    def live(c_ref, rows):
        sq_ref[0:1, :] = jnp.zeros((1, R), F32)
        sq_ref[0:1, 0:NO] = c_ref[...].astype(F32)
        counts = jnp.broadcast_to(sq_ref[0:1, :], (rows, R))
        return iota((rows, R), 0).astype(F32) < counts

    low = jnp.bitwise_xor(jnp.bitwise_and(src, 255), q * 64)
    low6_ref[...] = jnp.where(live(c6_ref, R), low.astype(F32), -1.0).astype(BF)
    hi6_ref[...] = jnp.right_shift(src, 8).astype(F32).astype(BF)
    a5 = a5_ref[...]
    sq_ref[0:16, 0:NO] = (block(jnp.right_shift(a5, 3)) + jnp.bitwise_and(a5, 7)).astype(F32)
    code5 = sq_ref[0:16, :]
    code5 = jnp.where(live(c5_ref, 16), code5, -1.0)
    sq_ref[0:2, 0:NO] = (block(a4_ref[...]) + 8).astype(F32)
    code4 = sq_ref[0:16, :]
    code4 = jnp.where(live(c4_ref, 16), code4, -1.0)
    code = jnp.concatenate([code5, code4], axis=0)
    upper = code >= 256.0
    low54_ref[...] = jnp.where(upper, code - 256.0, code).astype(BF)
    hi54_ref[...] = upper.astype(F32).astype(BF)
    sq_ref[...] = jnp.full((R, R), -1.0, F32)
    sq_ref[0:16, 0:NO] = t5_ref[...].astype(F32)
    sq_ref[16:18, 0:NO] = t4_ref[...].astype(F32) + 32.0
    sq_ref[...] = sq_ref[...].T
    packed = sq_ref[pl.ds(0, 24, stride=4), :]
    lane = iota((24, R), 1)
    for i in range(1, 4):
        part = pltpu.roll(sq_ref[pl.ds(i, 24, stride=4), :], 32 * i, 1)
        packed = jnp.where(lane >= 32 * i, part, packed)
    t54_ref[...] = packed
    fetches[-1].wait()


def hot(column, rows):
    wide = jnp.broadcast_to(column, (rows, R))
    lane = iota((rows, R), 1)
    one = jnp.ones((rows, R), BF)
    zero = jnp.zeros((rows, R), BF)
    left = jnp.where(wide == lane.astype(BF), one, zero)
    right = jnp.where(wide == (lane + R).astype(BF), one, zero)
    return jnp.concatenate([left, right], axis=1)


def placing(row, rows):
    wide = jnp.broadcast_to(row, (rows, R)).astype(BF)
    down = iota((rows, R), 0).astype(BF)
    return jnp.where(wide == down, jnp.ones((rows, R), BF), jnp.zeros((rows, R), BF))


def fine_kernel(z_ref, g_ref, own_ref, prev_ref, next_ref, far_ref, t_ref, low_ref, hi_ref, tgt_ref, acc_ref, x_ref):
    z = z_ref[0]
    x_ref[:, R : 2 * R] = own_ref[0:256]

    g = g_ref[0]
    nothing = jnp.zeros((256, R), BF)

    @pl.when(z == 0)
    def _():
        x_ref[:, 0:R] = jnp.where(g > 0, far_ref[...], nothing)

    @pl.when(z > 0)
    def _():
        x_ref[:, 0:R] = prev_ref[0:256]

    @pl.when(z == 7)
    def _():
        x_ref[:, 2 * R : 3 * R] = jnp.where(g < 7, far_ref[...], nothing)

    @pl.when(z < 7)
    def _():
        x_ref[:, 2 * R : 3 * R] = next_ref[0:256]

    low = low_ref[...]
    hi = hi_ref[...]
    for first in range(0, NO, G):
        ops = range(first, min(first + G, NO))
        hots = jnp.concatenate([hot(low[:, o : o + 1], R) for o in ops], axis=0)
        found = jnp.dot(hots, x_ref[...], preferred_element_type=F32).astype(BF)
        ys, places = [], []
        for n, o in enumerate(ops):
            seg = jnp.broadcast_to(hi[:, o : o + 1], (R, R))
            p = found[n * R : (n + 1) * R]
            p = jnp.where(seg == jnp.asarray(0, BF), p[:, 0:R], jnp.where(seg == jnp.asarray(1, BF), p[:, R : 2 * R], p[:, 2 * R :]))
            ys.append(jnp.dot(p, t_ref[o], preferred_element_type=F32).astype(BF))
            places.append(placing(tgt_ref[o : o + 1, :], 256))
        added = jnp.dot(jnp.concatenate(places, axis=1), jnp.concatenate(ys, axis=0), preferred_element_type=F32)
        if first == 0:
            acc_ref[...] = added
        else:
            acc_ref[...] += added


def coarse_kernel(q_ref, acc_ref, both_ref, prev_ref, next_ref, p_ref, m_ref, t_ref, low_ref, hi_ref, t54_ref,
                  o0_ref, o1_ref, o2_ref, o3_ref, x_ref, far_ref):
    x_ref[0:64, 0:R] = both_ref[256:320]
    x_ref[64:128, 0:R] = next_ref[256:320]
    x_ref[128:192, 0:R] = m_ref[64:128]
    x_ref[192:256, 0:R] = m_ref[0:64]
    x_ref[0:64, R : 2 * R] = m_ref[128:192]
    x_ref[64:128, R : 2 * R] = p_ref[0:64]
    x_ref[128:192, R : 2 * R] = p_ref[64:128]
    x_ref[192:256, R : 2 * R] = prev_ref[256:320]
    low = low_ref[...]
    hi = hi_ref[...]
    for first in range(0, NO, NO):
        ops = range(first, min(first + NO, NO))
        hots = jnp.concatenate([hot(low[:, o : o + 1], 32) for o in ops], axis=0)
        found = jnp.dot(hots, x_ref[...], preferred_element_type=F32).astype(BF)
        ys = []
        for n, o in enumerate(ops):
            seg = jnp.broadcast_to(hi[:, o : o + 1], (32, R))
            p = found[n * 32 : (n + 1) * 32]
            p = jnp.where(seg == jnp.asarray(0, BF), p[:, 0:R], p[:, R:])
            ys.append(jnp.dot(p, t_ref[o], preferred_element_type=F32).astype(BF))
        short = -len(ops) % 4
        if short:
            ys.append(jnp.zeros((32 * short, R), BF))
        rows = range(first // 4, (first + len(ops) + 3) // 4)
        places = jnp.concatenate([placing(t54_ref[j : j + 1, :], 48) for j in rows], axis=1)
        added = jnp.dot(places, jnp.concatenate(ys, axis=0), preferred_element_type=F32)
        if first == 0:
            far_ref[...] = added
        else:
            far_ref[...] += added
    q = q_ref[0]
    far_ref[0:32] = far_ref[0:32] * 0.5
    far_ref[32:48] = far_ref[32:48] * 0.25
    for k, out in enumerate((o0_ref, o1_ref, o2_ref, o3_ref)):
        d = jnp.bitwise_xor(q, k)
        out[0:64] = acc_ref[pl.ds(64 * d, 64), :].astype(BF)
        five = far_ref[pl.ds(8 * d, 8), :]
        four = jnp.broadcast_to(far_ref[pl.ds(32 + d, 1), :], (8, R))
        small = jnp.concatenate([five, four], axis=0)
        top = small.astype(BF)
        out[64:80] = top
        out[80:96] = (small - top.astype(F32)).astype(BF)


def final_kernel(a_ref, b_ref, c_ref, d_ref, dn_ref, out_ref, s_ref):
    total = (a_ref[...].astype(F32) + b_ref[...].astype(F32)) + (c_ref[...].astype(F32) + d_ref[...].astype(F32))
    small = total[64:80] + total[80:96]
    far5 = small[0:8]
    local4 = small[8:16].astype(BF)
    row = iota((8, R), 0)
    local5 = far5
    for c in range(8):
        spread = jnp.dot(local4, dn_ref[c], preferred_element_type=F32)
        local5 = local5 + jnp.where(row == c, spread, 0.0)
    local5 = local5.astype(BF)
    for c in range(8):
        s_ref[pl.ds(c, 8, stride=8), :] = jnp.dot(local5, dn_ref[c], preferred_element_type=F32)
    out_ref[...] = (total[0:64] + s_ref[...]).astype(BF)


VM = pl.BlockSpec(memory_space=pltpu.VMEM)
SM = pl.BlockSpec(memory_space=pltpu.SMEM)
FAR = pl.BlockSpec(memory_space=pl.ANY)
LIMIT = pltpu.CompilerParams(vmem_limit_bytes=24 * 1024 * 1024)


def near_core(value):
    return pltpu.with_memory_space_constraint(value, pltpu.VMEM)


def in_hbm(value):
    return pltpu.with_memory_space_constraint(value, pltpu.HBM)


def call(kernel, outs, scratch, vectors, scalars=(), far=0):
    return pl.pallas_call(
        kernel,
        out_shape=tuple(pltpu.VMEM(dims, kind) for dims, kind in outs),
        in_specs=[SM] * len(scalars) + [VM] * (len(vectors) - far) + [FAR] * far,
        out_specs=tuple([VM] * len(outs)),
        scratch_shapes=scratch,
        compiler_params=LIMIT,
    )(*scalars, *vectors)


SUB = ("x", "c")
MORTON = ("g", "z")


def rows_of(table):
    return table.transpose(1, 0, 2)


def crossed(value, k):
    return lax.ppermute(value, SUB, [(i, i ^ k) for i in range(4)])


def local(multipoles, translations, upward_ops, downward_ops, targets_l6, source_boxes_level6, counts_l6,
          target_boxes_level5, anchors_l5, counts_l5, targets_l4, anchors_l4, counts_l4):
    q = lax.axis_index(SUB).astype(jnp.int32).reshape(1)
    z = lax.axis_index("z").astype(jnp.int32).reshape(1)
    g = lax.axis_index("g").astype(jnp.int32).reshape(1)
    groups, ring = lax.axis_size("g"), lax.axis_size("z")
    ends = [(i * ring + ring - 1, i * ring + ring) for i in range(groups - 1)]
    ends = dict(ends + [(j, i) for i, j in ends])

    (pack,) = call(upward_kernel, [((80, R), BF)], [pltpu.VMEM((64, R), F32)], [in_hbm(multipoles), in_hbm(upward_ops)])
    peers = [crossed(pack, k) for k in (1, 2, 3)]
    low6, hi6, low54, hi54, t54, tgt, both, held = call(
        prep_kernel,
        [((R, R), BF), ((R, R), BF), ((32, R), BF), ((32, R), BF), ((24, R), F32), ((80, R), F32),
         ((320, R), BF), ((NO, R, R), BF)],
        [pltpu.VMEM((R, R), F32),
         pltpu.VMEM((NO, 1, R), jnp.int32), pltpu.VMEM((1, NO), jnp.int32), pltpu.VMEM((16, NO), jnp.int32),
         pltpu.VMEM((1, NO), jnp.int32), pltpu.VMEM((2, NO), jnp.int32), pltpu.VMEM((1, NO), jnp.int32),
         pltpu.VMEM((16, NO), jnp.int32), pltpu.VMEM((2, NO), jnp.int32), pltpu.VMEM((NO, 1, R), jnp.int32),
         pltpu.SemaphoreType.DMA((10,))],
        [near_core(pack), *map(in_hbm, (rows_of(source_boxes_level6), counts_l6, anchors_l5[0].T, counts_l5,
                       anchors_l4[0].T, counts_l4, target_boxes_level5[0].T, targets_l4[0].T, rows_of(targets_l6), translations))],
        [4 * z + q], far=10)
    for k, peer in enumerate(peers):
        both = lax.dynamic_update_slice(both, peer[0:64], (64 * k + 64, 0))
        both = lax.dynamic_update_slice(both, peer[64:80], (16 * k + 272, 0))

    def shifted(value, by):
        return lax.ppermute(value, "z", [(i, (i + by) % ring) for i in range(ring)])

    before = shifted(both, 1)
    after = shifted(both, -1)
    far = lax.ppermute(both[0:256], MORTON, [(i, ends.get(i, i)) for i in range(groups * ring)])
    pair = jnp.concatenate([both[256:320], after[256:320]], axis=0)
    three = jnp.concatenate([both[256:320], before[256:320], after[256:320]], axis=0)
    minus = shifted(three, -3)
    plus = shifted(pair, 3)
    (fine,) = call(fine_kernel, [((256, R), F32)], [pltpu.VMEM((256, 3 * R), BF)],
                   [*map(near_core, (both, before, after, far, held, low6, hi6, tgt))], [z, g])
    parts = call(coarse_kernel, [((96, R), BF)] * 4, [pltpu.VMEM((256, 2 * R), BF), pltpu.VMEM((48, R), F32)],
                 [*map(near_core, (fine, both, before, after, plus, minus, held, low54, hi54, t54))], [q])
    received = [crossed(parts[k], k) for k in (1, 2, 3)]
    return pl.pallas_call(
        final_kernel,
        out_shape=jax.ShapeDtypeStruct((64, R), BF),
        in_specs=[VM] * 5,
        out_specs=VM,
        scratch_shapes=[pltpu.VMEM((64, R), F32)],
        compiler_params=LIMIT,
        name="downward",
    )(*[near_core(v) for v in (parts[0], *received, downward_ops)])


def solution(mesh):
    cut = Mesh(mesh.devices.reshape(8, 8, 2, 2), ("g", "z", "x", "c"))
    both = MORTON + SUB
    placed = (
        P(both, None),
        P(SUB, None, None),
        P(),
        P(),
        P(MORTON, SUB, None),
        P(MORTON, SUB, None),
        P(MORTON, SUB),
        P(MORTON, SUB, None),
        P(MORTON, SUB, None),
        P(MORTON, SUB),
        P(MORTON, SUB, None),
        P(MORTON, SUB, None),
        P(MORTON, SUB),
    )
    return jax.shard_map(local, mesh=cut, in_specs=placed, out_specs=P(both, None), check_vma=False)
```

```python
import jax
import jax.numpy as jnp
from jax import lax
from jax.experimental import pallas as pl
from jax.experimental.pallas import tpu as pltpu
from jax.sharding import Mesh
from jax.sharding import PartitionSpec as P


R = 128
NO = 79
G = 20
BF = jnp.bfloat16
F32 = jnp.float32


def iota(shape, dim):
    return lax.broadcasted_iota(jnp.int32, shape, dim)


def upward_kernel(m_ref, p1_ref, p2_ref, p3_ref, up_ref, both_ref, st_ref, five_ref):
    for k, piece in enumerate((m_ref, p1_ref, p2_ref, p3_ref)):
        both_ref[64 * k : 64 * k + 64] = piece[...]
        st_ref[64 * k : 64 * k + 64] = piece[...].astype(F32)
    c5 = jnp.zeros((32, R), F32)
    for c in range(8):
        rows = st_ref[pl.ds(c, 32, stride=8), :].astype(BF)
        c5 = c5 + jnp.dot(rows, up_ref[c], preferred_element_type=F32)
    c5 = c5.astype(BF)
    five_ref[...] = c5.astype(F32)
    c4 = jnp.zeros((8, R), F32)
    for c in range(8):
        rows = five_ref[pl.ds(c, 4, stride=8), :]
        rows = jnp.concatenate([rows, rows], axis=0).astype(BF)
        c4 = c4 + jnp.dot(rows, up_ref[c], preferred_element_type=F32)
    both_ref[256:288] = c5
    both_ref[288:304] = jnp.concatenate([c4, c4], axis=0).astype(BF)


def prep_kernel(i_ref, m_hbm, up_hbm, src_hbm, c6_hbm, a5_hbm, c5_hbm, a4_hbm, c4_hbm, t5_hbm, t4_hbm, t6_hbm, t_hbm,
                low6_ref, hi6_ref, low54_ref, hi54_ref, t54_ref, tgt_ref, m_ref, up_ref, t_ref, sq_ref,
                src_ref, c6_ref, a5_ref, c5_ref, a4_ref, c4_ref, t5_ref, t4_ref, t6_ref, sems):
    pairs = ((src_hbm, src_ref), (c6_hbm, c6_ref), (a5_hbm, a5_ref), (c5_hbm, c5_ref),
             (a4_hbm, a4_ref), (c4_hbm, c4_ref), (t5_hbm, t5_ref), (t4_hbm, t4_ref), (t6_hbm, t6_ref),
             (m_hbm, m_ref), (up_hbm, up_ref), (t_hbm, t_ref))
    fetches = [pltpu.make_async_copy(source, place, sems.at[i]) for i, (source, place) in enumerate(pairs)]
    for fetch in fetches:
        fetch.start()
    for fetch in fetches[:-3]:
        fetch.wait()
    i = i_ref[0]
    q = jnp.bitwise_and(i, 3)
    z = jnp.right_shift(i, 2)

    def block(d, rows):
        ahead = jnp.bitwise_and(jnp.right_shift(d, 2) - z, 7)
        place = 256 * jnp.right_shift(ahead, 2) + 48 * jnp.bitwise_and(ahead, 3)
        return place + rows * jnp.bitwise_xor(jnp.bitwise_and(d, 3), q)

    tgt_ref[0:NO, :] = t6_ref[...].reshape(NO, R).astype(F32)
    tgt_ref[NO:80, :] = jnp.zeros((80 - NO, R), F32)

    sq_ref[...] = jnp.zeros((R, R), F32)
    sq_ref[0:NO, :] = src_ref[...].reshape(NO, R).astype(F32)
    src = sq_ref[...].T.astype(jnp.int32)

    def live(c_ref, rows):
        sq_ref[0:1, :] = jnp.zeros((1, R), F32)
        sq_ref[0:1, 0:NO] = c_ref[...].astype(F32)
        counts = jnp.broadcast_to(sq_ref[0:1, :], (rows, R))
        return iota((rows, R), 0).astype(F32) < counts

    low = jnp.bitwise_xor(jnp.bitwise_and(src, 255), q * 64)
    low6_ref[...] = jnp.where(live(c6_ref, R), low.astype(F32), -1.0).astype(BF)
    hi6_ref[...] = jnp.right_shift(src, 8).astype(F32).astype(BF)
    a5 = a5_ref[...]
    sq_ref[0:16, 0:NO] = (block(jnp.right_shift(a5, 3), 8) + jnp.bitwise_and(a5, 7)).astype(F32)
    code5 = sq_ref[0:16, :]
    code5 = jnp.where(live(c5_ref, 16), code5, -1.0)
    sq_ref[0:2, 0:NO] = (block(a4_ref[...], 1) + 32).astype(F32)
    code4 = sq_ref[0:16, :]
    code4 = jnp.where(live(c4_ref, 16), code4, -1.0)
    code = jnp.concatenate([code5, code4], axis=0)
    upper = code >= 256.0
    low54_ref[...] = jnp.where(upper, code - 256.0, code).astype(BF)
    hi54_ref[...] = upper.astype(F32).astype(BF)
    sq_ref[...] = jnp.full((R, R), -1.0, F32)
    sq_ref[0:16, 0:NO] = t5_ref[...].astype(F32)
    sq_ref[16:18, 0:NO] = t4_ref[...].astype(F32) + 32.0
    sq_ref[...] = sq_ref[...].T
    packed = sq_ref[pl.ds(0, 24, stride=4), :]
    lane = iota((24, R), 1)
    for i in range(1, 4):
        part = pltpu.roll(sq_ref[pl.ds(i, 24, stride=4), :], 32 * i, 1)
        packed = jnp.where(lane >= 32 * i, part, packed)
    t54_ref[...] = packed
    for fetch in fetches[-3:]:
        fetch.wait()


def hot(column, rows):
    wide = jnp.broadcast_to(column, (rows, R))
    lane = iota((rows, R), 1)
    one = jnp.ones((rows, R), BF)
    zero = jnp.zeros((rows, R), BF)
    left = jnp.where(wide == lane.astype(BF), one, zero)
    right = jnp.where(wide == (lane + R).astype(BF), one, zero)
    return jnp.concatenate([left, right], axis=1)


def placing(row, rows):
    wide = jnp.broadcast_to(row, (rows, R)).astype(BF)
    down = iota((rows, R), 0).astype(BF)
    return jnp.where(wide == down, jnp.ones((rows, R), BF), jnp.zeros((rows, R), BF))


def fine_kernel(z_ref, g_ref, own_ref, prev_ref, next_ref, far_ref, t_ref, low_ref, hi_ref, tgt_ref, acc_ref, x_ref):
    z = z_ref[0]
    x_ref[:, R : 2 * R] = own_ref[0:256]

    g = g_ref[0]
    nothing = jnp.zeros((256, R), BF)

    @pl.when(z == 0)
    def _():
        x_ref[:, 0:R] = jnp.where(g > 0, far_ref[...], nothing)

    @pl.when(z > 0)
    def _():
        x_ref[:, 0:R] = prev_ref[0:256]

    @pl.when(z == 7)
    def _():
        x_ref[:, 2 * R : 3 * R] = jnp.where(g < 7, far_ref[...], nothing)

    @pl.when(z < 7)
    def _():
        x_ref[:, 2 * R : 3 * R] = next_ref[0:256]

    low = low_ref[...]
    hi = hi_ref[...]
    for first in range(0, NO, G):
        ops = range(first, min(first + G, NO))
        hots = jnp.concatenate([hot(low[:, o : o + 1], R) for o in ops], axis=0)
        found = jnp.dot(hots, x_ref[...], preferred_element_type=F32).astype(BF)
        ys, places = [], []
        for n, o in enumerate(ops):
            seg = jnp.broadcast_to(hi[:, o : o + 1], (R, R))
            p = found[n * R : (n + 1) * R]
            p = jnp.where(seg == jnp.asarray(0, BF), p[:, 0:R], jnp.where(seg == jnp.asarray(1, BF), p[:, R : 2 * R], p[:, 2 * R :]))
            ys.append(jnp.dot(p, t_ref[o], preferred_element_type=F32).astype(BF))
            places.append(placing(tgt_ref[o : o + 1, :], 256))
        added = jnp.dot(jnp.concatenate(places, axis=1), jnp.concatenate(ys, axis=0), preferred_element_type=F32)
        if first == 0:
            acc_ref[...] = added
        else:
            acc_ref[...] += added


def coarse_kernel(q_ref, acc_ref, both_ref, prev_ref, next_ref, p_ref, m_ref, t_ref, low_ref, hi_ref, t54_ref,
                  o0_ref, o1_ref, o2_ref, o3_ref, x_ref, far_ref):
    x_ref[0:48, 0:R] = both_ref[256:304]
    x_ref[48:96, 0:R] = next_ref[256:304]
    x_ref[96:144, 0:R] = m_ref[48:96]
    x_ref[144:192, 0:R] = m_ref[0:48]
    x_ref[0:48, R : 2 * R] = m_ref[96:144]
    x_ref[48:96, R : 2 * R] = p_ref[0:48]
    x_ref[96:144, R : 2 * R] = p_ref[48:96]
    x_ref[144:192, R : 2 * R] = prev_ref[256:304]
    x_ref[192:256, :] = jnp.zeros((64, 2 * R), BF)
    low = low_ref[...]
    hi = hi_ref[...]
    for first in range(0, NO, NO):
        ops = range(first, min(first + NO, NO))
        hots = jnp.concatenate([hot(low[:, o : o + 1], 32) for o in ops], axis=0)
        found = jnp.dot(hots, x_ref[...], preferred_element_type=F32).astype(BF)
        ys = []
        for n, o in enumerate(ops):
            seg = jnp.broadcast_to(hi[:, o : o + 1], (32, R))
            p = found[n * 32 : (n + 1) * 32]
            p = jnp.where(seg == jnp.asarray(0, BF), p[:, 0:R], p[:, R:])
            ys.append(jnp.dot(p, t_ref[o], preferred_element_type=F32).astype(BF))
        short = -len(ops) % 4
        if short:
            ys.append(jnp.zeros((32 * short, R), BF))
        rows = range(first // 4, (first + len(ops) + 3) // 4)
        places = jnp.concatenate([placing(t54_ref[j : j + 1, :], 48) for j in rows], axis=1)
        added = jnp.dot(places, jnp.concatenate(ys, axis=0), preferred_element_type=F32)
        if first == 0:
            far_ref[...] = added
        else:
            far_ref[...] += added
    q = q_ref[0]
    far_ref[0:32] = far_ref[0:32] * 0.5
    far_ref[32:48] = far_ref[32:48] * 0.25
    for k, out in enumerate((o0_ref, o1_ref, o2_ref, o3_ref)):
        d = jnp.bitwise_xor(q, k)
        out[0:64] = acc_ref[pl.ds(64 * d, 64), :].astype(BF)
        five = far_ref[pl.ds(8 * d, 8), :]
        four = jnp.broadcast_to(far_ref[pl.ds(32 + d, 1), :], (8, R))
        small = jnp.concatenate([five, four], axis=0)
        top = small.astype(BF)
        out[64:80] = top
        out[80:96] = (small - top.astype(F32)).astype(BF)


def final_kernel(a_ref, b_ref, c_ref, d_ref, dn_ref, out_ref, s_ref):
    total = (a_ref[...].astype(F32) + b_ref[...].astype(F32)) + (c_ref[...].astype(F32) + d_ref[...].astype(F32))
    small = total[64:80] + total[80:96]
    far5 = small[0:8]
    local4 = small[8:16].astype(BF)
    row = iota((8, R), 0)
    local5 = far5
    for c in range(8):
        spread = jnp.dot(local4, dn_ref[c], preferred_element_type=F32)
        local5 = local5 + jnp.where(row == c, spread, 0.0)
    local5 = local5.astype(BF)
    for c in range(8):
        s_ref[pl.ds(c, 8, stride=8), :] = jnp.dot(local5, dn_ref[c], preferred_element_type=F32)
    out_ref[...] = (total[0:64] + s_ref[...]).astype(BF)


VM = pl.BlockSpec(memory_space=pltpu.VMEM)
SM = pl.BlockSpec(memory_space=pltpu.SMEM)
FAR = pl.BlockSpec(memory_space=pl.ANY)
LIMIT = pltpu.CompilerParams(vmem_limit_bytes=24 * 1024 * 1024)


def near_core(value):
    return pltpu.with_memory_space_constraint(value, pltpu.VMEM)


def in_hbm(value):
    return pltpu.with_memory_space_constraint(value, pltpu.HBM)


def call(kernel, outs, scratch, vectors, scalars=(), far=0):
    return pl.pallas_call(
        kernel,
        out_shape=tuple(pltpu.VMEM(dims, kind) for dims, kind in outs),
        in_specs=[SM] * len(scalars) + [VM] * (len(vectors) - far) + [FAR] * far,
        out_specs=tuple([VM] * len(outs)),
        scratch_shapes=scratch,
        compiler_params=LIMIT,
    )(*scalars, *vectors)


SUB = ("x", "c")
MORTON = ("g", "z")


def rows_of(table):
    return table.transpose(1, 0, 2)


def crossed(value, k):
    return lax.ppermute(value, SUB, [(i, i ^ k) for i in range(4)])


def local(multipoles, translations, upward_ops, downward_ops, targets_l6, source_boxes_level6, counts_l6,
          target_boxes_level5, anchors_l5, counts_l5, targets_l4, anchors_l4, counts_l4):
    q = lax.axis_index(SUB).astype(jnp.int32).reshape(1)
    z = lax.axis_index("z").astype(jnp.int32).reshape(1)
    g = lax.axis_index("g").astype(jnp.int32).reshape(1)
    groups, ring = lax.axis_size("g"), lax.axis_size("z")
    ends = [(i * ring + ring - 1, i * ring + ring) for i in range(groups - 1)]
    ends = dict(ends + [(j, i) for i, j in ends])

    peers = [crossed(multipoles, k) for k in (1, 2, 3)]
    low6, hi6, low54, hi54, t54, tgt, mine, up, held = call(
        prep_kernel,
        [((R, R), BF), ((R, R), BF), ((32, R), BF), ((32, R), BF), ((24, R), F32), ((80, R), F32),
         ((64, R), BF), ((8, R, R), BF), ((NO, R, R), BF)],
        [pltpu.VMEM((R, R), F32),
         pltpu.VMEM((NO, 1, R), jnp.int32), pltpu.VMEM((1, NO), jnp.int32), pltpu.VMEM((16, NO), jnp.int32),
         pltpu.VMEM((1, NO), jnp.int32), pltpu.VMEM((2, NO), jnp.int32), pltpu.VMEM((1, NO), jnp.int32),
         pltpu.VMEM((16, NO), jnp.int32), pltpu.VMEM((2, NO), jnp.int32), pltpu.VMEM((NO, 1, R), jnp.int32),
         pltpu.SemaphoreType.DMA((12,))],
        [*map(in_hbm, (multipoles, upward_ops, rows_of(source_boxes_level6), counts_l6, anchors_l5[0].T, counts_l5,
                       anchors_l4[0].T, counts_l4, target_boxes_level5[0].T, targets_l4[0].T, rows_of(targets_l6), translations))],
        [4 * z + q], far=12)
    (both,) = call(upward_kernel, [((304, R), BF)], [pltpu.VMEM((256, R), F32), pltpu.VMEM((32, R), F32)],
                   [*map(near_core, (mine, *peers, up))])

    def shifted(value, by):
        return lax.ppermute(value, "z", [(i, (i + by) % ring) for i in range(ring)])

    before = shifted(both, 1)
    after = shifted(both, -1)
    far = lax.ppermute(both[0:256], MORTON, [(i, ends.get(i, i)) for i in range(groups * ring)])
    pair = jnp.concatenate([both[256:304], after[256:304]], axis=0)
    three = jnp.concatenate([both[256:304], before[256:304], after[256:304]], axis=0)
    minus = shifted(three, -3)
    plus = shifted(pair, 3)
    (fine,) = call(fine_kernel, [((256, R), F32)], [pltpu.VMEM((256, 3 * R), BF)],
                   [*map(near_core, (both, before, after, far, held, low6, hi6, tgt))], [z, g])
    parts = call(coarse_kernel, [((96, R), BF)] * 4, [pltpu.VMEM((256, 2 * R), BF), pltpu.VMEM((48, R), F32)],
                 [*map(near_core, (fine, both, before, after, plus, minus, held, low54, hi54, t54))], [q])
    received = [crossed(parts[k], k) for k in (1, 2, 3)]
    return pl.pallas_call(
        final_kernel,
        out_shape=jax.ShapeDtypeStruct((64, R), BF),
        in_specs=[VM] * 5,
        out_specs=VM,
        scratch_shapes=[pltpu.VMEM((64, R), F32)],
        compiler_params=LIMIT,
        name="downward",
    )(*[near_core(v) for v in (parts[0], *received, downward_ops)])


def solution(mesh):
    cut = Mesh(mesh.devices.reshape(8, 8, 2, 2), ("g", "z", "x", "c"))
    both = MORTON + SUB
    placed = (
        P(both, None),
        P(SUB, None, None),
        P(),
        P(),
        P(MORTON, SUB, None),
        P(MORTON, SUB, None),
        P(MORTON, SUB),
        P(MORTON, SUB, None),
        P(MORTON, SUB, None),
        P(MORTON, SUB),
        P(MORTON, SUB, None),
        P(MORTON, SUB, None),
        P(MORTON, SUB),
    )
    return jax.shard_map(local, mesh=cut, in_specs=placed, out_specs=P(both, None), check_vma=False)
```

```python
import jax
import jax.numpy as jnp
from jax import lax
from jax.experimental import pallas as pl
from jax.experimental.pallas import tpu as pltpu
from jax.sharding import Mesh
from jax.sharding import PartitionSpec as P


R = 128
NO = 79
G = 20
BF = jnp.bfloat16
F32 = jnp.float32


def iota(shape, dim):
    return lax.broadcasted_iota(jnp.int32, shape, dim)


def upward_kernel(m_ref, p1_ref, p2_ref, p3_ref, up_ref, both_ref, st_ref, five_ref):
    for k, piece in enumerate((m_ref, p1_ref, p2_ref, p3_ref)):
        both_ref[64 * k : 64 * k + 64] = piece[...]
        st_ref[64 * k : 64 * k + 64] = piece[...].astype(F32)
    c5 = jnp.zeros((32, R), F32)
    for c in range(8):
        rows = st_ref[pl.ds(c, 32, stride=8), :].astype(BF)
        c5 = c5 + jnp.dot(rows, up_ref[c], preferred_element_type=F32)
    c5 = c5.astype(BF)
    five_ref[...] = c5.astype(F32)
    c4 = jnp.zeros((8, R), F32)
    for c in range(8):
        rows = five_ref[pl.ds(c, 4, stride=8), :]
        rows = jnp.concatenate([rows, rows], axis=0).astype(BF)
        c4 = c4 + jnp.dot(rows, up_ref[c], preferred_element_type=F32)
    both_ref[256:288] = c5
    both_ref[288:304] = jnp.concatenate([c4, c4], axis=0).astype(BF)


def prep_kernel(i_ref, m_hbm, up_hbm, src_hbm, c6_hbm, a5_hbm, c5_hbm, a4_hbm, c4_hbm, t5_hbm, t4_hbm, t6_hbm, t_hbm,
                low6_ref, hi6_ref, low54_ref, hi54_ref, t54_ref, tgt_ref, m_ref, up_ref, t_ref, sq_ref,
                src_ref, c6_ref, a5_ref, c5_ref, a4_ref, c4_ref, t5_ref, t4_ref, t6_ref, sems):
    pairs = ((src_hbm, src_ref), (c6_hbm, c6_ref), (a5_hbm, a5_ref), (c5_hbm, c5_ref),
             (a4_hbm, a4_ref), (c4_hbm, c4_ref), (t5_hbm, t5_ref), (t4_hbm, t4_ref), (t6_hbm, t6_ref),
             (m_hbm, m_ref), (up_hbm, up_ref), (t_hbm, t_ref))
    fetches = [pltpu.make_async_copy(source, place, sems.at[i]) for i, (source, place) in enumerate(pairs)]
    for fetch in fetches:
        fetch.start()
    for fetch in fetches[:-3]:
        fetch.wait()
    i = i_ref[0]
    q = jnp.bitwise_and(i, 3)
    z = jnp.right_shift(i, 2)

    def block(d, rows):
        ahead = jnp.bitwise_and(jnp.right_shift(d, 2) - z, 7)
        place = 256 * jnp.right_shift(ahead, 2) + 48 * jnp.bitwise_and(ahead, 3)
        return place + rows * jnp.bitwise_xor(jnp.bitwise_and(d, 3), q)

    tgt_ref[0:NO, :] = t6_ref[...].reshape(NO, R).astype(F32)
    tgt_ref[NO:80, :] = jnp.zeros((80 - NO, R), F32)

    sq_ref[...] = jnp.zeros((R, R), F32)
    sq_ref[0:NO, :] = src_ref[...].reshape(NO, R).astype(F32)
    src = sq_ref[...].T.astype(jnp.int32)

    def live(c_ref, rows):
        sq_ref[0:1, :] = jnp.zeros((1, R), F32)
        sq_ref[0:1, 0:NO] = c_ref[...].astype(F32)
        counts = jnp.broadcast_to(sq_ref[0:1, :], (rows, R))
        return iota((rows, R), 0).astype(F32) < counts

    low = jnp.bitwise_xor(jnp.bitwise_and(src, 255), q * 64)
    low6_ref[...] = jnp.where(live(c6_ref, R), low.astype(F32), -1.0).astype(BF)
    hi6_ref[...] = jnp.right_shift(src, 8).astype(F32).astype(BF)
    a5 = a5_ref[...]
    sq_ref[0:16, 0:NO] = (block(jnp.right_shift(a5, 3), 8) + jnp.bitwise_and(a5, 7)).astype(F32)
    code5 = sq_ref[0:16, :]
    code5 = jnp.where(live(c5_ref, 16), code5, -1.0)
    sq_ref[0:2, 0:NO] = (block(a4_ref[...], 1) + 32).astype(F32)
    code4 = sq_ref[0:16, :]
    code4 = jnp.where(live(c4_ref, 16), code4, -1.0)
    code = jnp.concatenate([code5, code4], axis=0)
    upper = code >= 256.0
    low54_ref[...] = jnp.where(upper, code - 256.0, code).astype(BF)
    hi54_ref[...] = upper.astype(F32).astype(BF)
    sq_ref[...] = jnp.full((R, R), -1.0, F32)
    sq_ref[0:16, 0:NO] = t5_ref[...].astype(F32)
    sq_ref[16:18, 0:NO] = t4_ref[...].astype(F32) + 32.0
    sq_ref[...] = sq_ref[...].T
    packed = sq_ref[pl.ds(0, 24, stride=4), :]
    lane = iota((24, R), 1)
    for i in range(1, 4):
        part = pltpu.roll(sq_ref[pl.ds(i, 24, stride=4), :], 32 * i, 1)
        packed = jnp.where(lane >= 32 * i, part, packed)
    t54_ref[...] = packed
    for fetch in fetches[-3:]:
        fetch.wait()


def hot(column, rows):
    wide = jnp.broadcast_to(column, (rows, R))
    lane = iota((rows, R), 1)
    one = jnp.ones((rows, R), BF)
    zero = jnp.zeros((rows, R), BF)
    left = jnp.where(wide == lane.astype(BF), one, zero)
    right = jnp.where(wide == (lane + R).astype(BF), one, zero)
    return jnp.concatenate([left, right], axis=1)


def placing(row, rows):
    wide = jnp.broadcast_to(row, (rows, R)).astype(BF)
    down = iota((rows, R), 0).astype(BF)
    return jnp.where(wide == down, jnp.ones((rows, R), BF), jnp.zeros((rows, R), BF))


def fine_kernel(z_ref, g_ref, own_ref, prev_ref, next_ref, far_ref, t_ref, low_ref, hi_ref, tgt_ref, acc_ref, x_ref):
    z = z_ref[0]
    x_ref[:, R : 2 * R] = own_ref[0:256]

    g = g_ref[0]
    nothing = jnp.zeros((256, R), BF)

    @pl.when(z == 0)
    def _():
        x_ref[:, 0:R] = jnp.where(g > 0, far_ref[...], nothing)

    @pl.when(z > 0)
    def _():
        x_ref[:, 0:R] = prev_ref[0:256]

    @pl.when(z == 7)
    def _():
        x_ref[:, 2 * R : 3 * R] = jnp.where(g < 7, far_ref[...], nothing)

    @pl.when(z < 7)
    def _():
        x_ref[:, 2 * R : 3 * R] = next_ref[0:256]

    low = low_ref[...]
    hi = hi_ref[...]
    for first in range(0, NO, G):
        ops = range(first, min(first + G, NO))
        hots = jnp.concatenate([hot(low[:, o : o + 1], R) for o in ops], axis=0)
        found = jnp.dot(hots, x_ref[...], preferred_element_type=F32).astype(BF)
        ys, places = [], []
        for n, o in enumerate(ops):
            seg = jnp.broadcast_to(hi[:, o : o + 1], (R, R))
            p = found[n * R : (n + 1) * R]
            p = jnp.where(seg == jnp.asarray(0, BF), p[:, 0:R], jnp.where(seg == jnp.asarray(1, BF), p[:, R : 2 * R], p[:, 2 * R :]))
            ys.append(jnp.dot(p, t_ref[o], preferred_element_type=F32).astype(BF))
            places.append(placing(tgt_ref[o : o + 1, :], 256))
        added = jnp.dot(jnp.concatenate(places, axis=1), jnp.concatenate(ys, axis=0), preferred_element_type=F32)
        if first == 0:
            acc_ref[...] = added
        else:
            acc_ref[...] += added


def coarse_kernel(q_ref, acc_ref, both_ref, prev_ref, next_ref, p_ref, m_ref, t_ref, low_ref, hi_ref, t54_ref,
                  o0_ref, o1_ref, o2_ref, o3_ref, x_ref, far_ref):
    x_ref[0:48, 0:R] = both_ref[256:304]
    x_ref[48:96, 0:R] = next_ref[256:304]
    x_ref[96:144, 0:R] = m_ref[48:96]
    x_ref[144:192, 0:R] = m_ref[0:48]
    x_ref[0:48, R : 2 * R] = m_ref[96:144]
    x_ref[48:96, R : 2 * R] = p_ref[0:48]
    x_ref[96:144, R : 2 * R] = p_ref[48:96]
    x_ref[144:192, R : 2 * R] = prev_ref[256:304]
    x_ref[192:256, :] = jnp.zeros((64, 2 * R), BF)
    low = low_ref[...]
    hi = hi_ref[...]
    for first in range(0, NO, NO):
        ops = range(first, min(first + NO, NO))
        hots = jnp.concatenate([hot(low[:, o : o + 1], 32) for o in ops], axis=0)
        found = jnp.dot(hots, x_ref[...], preferred_element_type=F32).astype(BF)
        ys = []
        for n, o in enumerate(ops):
            seg = jnp.broadcast_to(hi[:, o : o + 1], (32, R))
            p = found[n * 32 : (n + 1) * 32]
            p = jnp.where(seg == jnp.asarray(0, BF), p[:, 0:R], p[:, R:])
            ys.append(jnp.dot(p, t_ref[o], preferred_element_type=F32).astype(BF))
        short = -len(ops) % 4
        if short:
            ys.append(jnp.zeros((32 * short, R), BF))
        rows = range(first // 4, (first + len(ops) + 3) // 4)
        places = jnp.concatenate([placing(t54_ref[j : j + 1, :], 48) for j in rows], axis=1)
        added = jnp.dot(places, jnp.concatenate(ys, axis=0), preferred_element_type=F32)
        if first == 0:
            far_ref[...] = added
        else:
            far_ref[...] += added
    q = q_ref[0]
    far_ref[0:32] = far_ref[0:32] * 0.5
    far_ref[32:48] = far_ref[32:48] * 0.25
    for k, out in enumerate((o0_ref, o1_ref, o2_ref, o3_ref)):
        d = jnp.bitwise_xor(q, k)
        out[0:64] = acc_ref[pl.ds(64 * d, 64), :].astype(BF)
        five = far_ref[pl.ds(8 * d, 8), :]
        four = jnp.broadcast_to(far_ref[pl.ds(32 + d, 1), :], (8, R))
        small = jnp.concatenate([five, four], axis=0)
        top = small.astype(BF)
        out[64:80] = top
        out[80:96] = (small - top.astype(F32)).astype(BF)


def final_kernel(a_ref, b_ref, c_ref, d_ref, dn_ref, out_ref, s_ref):
    total = (a_ref[...].astype(F32) + b_ref[...].astype(F32)) + (c_ref[...].astype(F32) + d_ref[...].astype(F32))
    small = total[64:80] + total[80:96]
    far5 = small[0:8]
    local4 = small[8:16].astype(BF)
    row = iota((8, R), 0)
    local5 = far5
    for c in range(8):
        spread = jnp.dot(local4, dn_ref[c], preferred_element_type=F32)
        local5 = local5 + jnp.where(row == c, spread, 0.0)
    local5 = local5.astype(BF)
    for c in range(8):
        s_ref[pl.ds(c, 8, stride=8), :] = jnp.dot(local5, dn_ref[c], preferred_element_type=F32)
    out_ref[...] = (total[0:64] + s_ref[...]).astype(BF)


VM = pl.BlockSpec(memory_space=pltpu.VMEM)
SM = pl.BlockSpec(memory_space=pltpu.SMEM)
FAR = pl.BlockSpec(memory_space=pl.ANY)
LIMIT = pltpu.CompilerParams(vmem_limit_bytes=24 * 1024 * 1024)


def near_core(value):
    return pltpu.with_memory_space_constraint(value, pltpu.VMEM)


def in_hbm(value):
    return pltpu.with_memory_space_constraint(value, pltpu.HBM)


def call(kernel, outs, scratch, vectors, scalars=(), far=0):
    return pl.pallas_call(
        kernel,
        out_shape=tuple(pltpu.VMEM(dims, kind) for dims, kind in outs),
        in_specs=[SM] * len(scalars) + [VM] * (len(vectors) - far) + [FAR] * far,
        out_specs=tuple([VM] * len(outs)),
        scratch_shapes=scratch,
        compiler_params=LIMIT,
    )(*scalars, *vectors)


SUB = ("x", "c")
MORTON = ("g", "z")


def rows_of(table):
    return table.transpose(1, 0, 2)


def crossed(value, k):
    return lax.ppermute(value, SUB, [(i, i ^ k) for i in range(4)])


def local(multipoles, translations, upward_ops, downward_ops, targets_l6, source_boxes_level6, counts_l6,
          target_boxes_level5, anchors_l5, counts_l5, targets_l4, anchors_l4, counts_l4):
    q = lax.axis_index(SUB).astype(jnp.int32).reshape(1)
    z = lax.axis_index("z").astype(jnp.int32).reshape(1)
    g = lax.axis_index("g").astype(jnp.int32).reshape(1)
    groups, ring = lax.axis_size("g"), lax.axis_size("z")
    ends = [(i * ring + ring - 1, i * ring + ring) for i in range(groups - 1)]
    ends = dict(ends + [(j, i) for i, j in ends])

    peers = []
    for k in (1, 2, 3):
        peers.append(crossed(multipoles, k))
    low6, hi6, low54, hi54, t54, tgt, mine, up, held = call(
        prep_kernel,
        [((R, R), BF), ((R, R), BF), ((32, R), BF), ((32, R), BF), ((24, R), F32), ((80, R), F32),
         ((64, R), BF), ((8, R, R), BF), ((NO, R, R), BF)],
        [pltpu.VMEM((R, R), F32),
         pltpu.VMEM((NO, 1, R), jnp.int32), pltpu.VMEM((1, NO), jnp.int32), pltpu.VMEM((16, NO), jnp.int32),
         pltpu.VMEM((1, NO), jnp.int32), pltpu.VMEM((2, NO), jnp.int32), pltpu.VMEM((1, NO), jnp.int32),
         pltpu.VMEM((16, NO), jnp.int32), pltpu.VMEM((2, NO), jnp.int32), pltpu.VMEM((NO, 1, R), jnp.int32),
         pltpu.SemaphoreType.DMA((12,))],
        [*map(in_hbm, (multipoles, upward_ops, rows_of(source_boxes_level6), counts_l6, anchors_l5[0].T, counts_l5,
                       anchors_l4[0].T, counts_l4, target_boxes_level5[0].T, targets_l4[0].T, rows_of(targets_l6), translations))],
        [4 * z + q], far=12)
    (both,) = call(upward_kernel, [((304, R), BF)], [pltpu.VMEM((256, R), F32), pltpu.VMEM((32, R), F32)],
                   [*map(near_core, (mine, *peers, up))])

    def shifted(value, by):
        return lax.ppermute(value, "z", [(i, (i + by) % ring) for i in range(ring)])

    before = shifted(both, 1)
    after = shifted(both, -1)
    far = lax.ppermute(both[0:256], MORTON, [(i, ends.get(i, i)) for i in range(groups * ring)])
    pair = jnp.concatenate([both[256:304], after[256:304]], axis=0)
    three = jnp.concatenate([both[256:304], before[256:304], after[256:304]], axis=0)
    minus = shifted(three, -3)
    plus = shifted(pair, 3)
    (fine,) = call(fine_kernel, [((256, R), F32)], [pltpu.VMEM((256, 3 * R), BF)],
                   [*map(near_core, (both, before, after, far, held, low6, hi6, tgt))], [z, g])
    parts = call(coarse_kernel, [((96, R), BF)] * 4, [pltpu.VMEM((256, 2 * R), BF), pltpu.VMEM((48, R), F32)],
                 [*map(near_core, (fine, both, before, after, plus, minus, held, low54, hi54, t54))], [q])
    received = []
    for k in (1, 2, 3):
        received.append(crossed(parts[k], k))
    return pl.pallas_call(
        final_kernel,
        out_shape=jax.ShapeDtypeStruct((64, R), BF),
        in_specs=[VM] * 5,
        out_specs=VM,
        scratch_shapes=[pltpu.VMEM((64, R), F32)],
        compiler_params=LIMIT,
        name="downward",
    )(*[near_core(v) for v in (parts[0], *received, downward_ops)])


def solution(mesh):
    cut = Mesh(mesh.devices.reshape(8, 8, 2, 2), ("g", "z", "x", "c"))
    both = MORTON + SUB
    placed = (
        P(both, None),
        P(SUB, None, None),
        P(),
        P(),
        P(MORTON, SUB, None),
        P(MORTON, SUB, None),
        P(MORTON, SUB),
        P(MORTON, SUB, None),
        P(MORTON, SUB, None),
        P(MORTON, SUB),
        P(MORTON, SUB, None),
        P(MORTON, SUB, None),
        P(MORTON, SUB),
    )
    return jax.shard_map(local, mesh=cut, in_specs=placed, out_specs=P(both, None), check_vma=False)
```

```python
import jax
import jax.numpy as jnp
from jax import lax
from jax.experimental import pallas as pl
from jax.experimental.pallas import tpu as pltpu
from jax.sharding import Mesh
from jax.sharding import PartitionSpec as P


R = 128
NO = 79
G = 20
BF = jnp.bfloat16
F32 = jnp.float32


def iota(shape, dim):
    return lax.broadcasted_iota(jnp.int32, shape, dim)


def upward_kernel(m_ref, p1_ref, p2_ref, p3_ref, up_ref, both_ref, st_ref, five_ref):
    for k, piece in enumerate((m_ref, p1_ref, p2_ref, p3_ref)):
        both_ref[64 * k : 64 * k + 64] = piece[...]
        st_ref[64 * k : 64 * k + 64] = piece[...].astype(F32)
    c5 = jnp.zeros((32, R), F32)
    for c in range(8):
        rows = st_ref[pl.ds(c, 32, stride=8), :].astype(BF)
        c5 = c5 + jnp.dot(rows, up_ref[c], preferred_element_type=F32)
    c5 = c5.astype(BF)
    five_ref[...] = c5.astype(F32)
    c4 = jnp.zeros((8, R), F32)
    for c in range(8):
        rows = five_ref[pl.ds(c, 4, stride=8), :]
        rows = jnp.concatenate([rows, rows], axis=0).astype(BF)
        c4 = c4 + jnp.dot(rows, up_ref[c], preferred_element_type=F32)
    both_ref[256:288] = c5
    both_ref[288:304] = jnp.concatenate([c4, c4], axis=0).astype(BF)


def prep_kernel(i_ref, m_hbm, up_hbm, src_hbm, c6_hbm, a5_hbm, c5_hbm, a4_hbm, c4_hbm, t5_hbm, t4_hbm, t6_hbm, t_hbm,
                low6_ref, hi6_ref, low54_ref, hi54_ref, t54_ref, tgt_ref, m_ref, up_ref, t_ref, sq_ref,
                src_ref, c6_ref, a5_ref, c5_ref, a4_ref, c4_ref, t5_ref, t4_ref, t6_ref, sems):
    pairs = ((src_hbm, src_ref), (c6_hbm, c6_ref), (a5_hbm, a5_ref), (c5_hbm, c5_ref),
             (a4_hbm, a4_ref), (c4_hbm, c4_ref), (t5_hbm, t5_ref), (t4_hbm, t4_ref), (t6_hbm, t6_ref),
             (m_hbm, m_ref), (up_hbm, up_ref), (t_hbm, t_ref))
    fetches = [pltpu.make_async_copy(source, place, sems.at[i]) for i, (source, place) in enumerate(pairs)]
    for fetch in fetches:
        fetch.start()
    for fetch in fetches[:-3]:
        fetch.wait()
    i = i_ref[0]
    q = jnp.bitwise_and(i, 3)
    z = jnp.right_shift(i, 2)

    def block(d, rows):
        ahead = jnp.bitwise_and(jnp.right_shift(d, 2) - z, 7)
        place = 256 * jnp.right_shift(ahead, 2) + 48 * jnp.bitwise_and(ahead, 3)
        return place + rows * jnp.bitwise_xor(jnp.bitwise_and(d, 3), q)

    tgt_ref[0:NO, :] = t6_ref[...].reshape(NO, R).astype(F32)
    tgt_ref[NO:80, :] = jnp.zeros((80 - NO, R), F32)

    sq_ref[...] = jnp.zeros((R, R), F32)
    sq_ref[0:NO, :] = src_ref[...].reshape(NO, R).astype(F32)
    src = sq_ref[...].T.astype(jnp.int32)

    def live(c_ref, rows):
        sq_ref[0:1, :] = jnp.zeros((1, R), F32)
        sq_ref[0:1, 0:NO] = c_ref[...].astype(F32)
        counts = jnp.broadcast_to(sq_ref[0:1, :], (rows, R))
        return iota((rows, R), 0).astype(F32) < counts

    low = jnp.bitwise_xor(jnp.bitwise_and(src, 255), q * 64)
    low6_ref[...] = jnp.where(live(c6_ref, R), low.astype(F32), -1.0).astype(BF)
    hi6_ref[...] = jnp.right_shift(src, 8).astype(F32).astype(BF)
    a5 = a5_ref[...]
    sq_ref[0:16, 0:NO] = (block(jnp.right_shift(a5, 3), 8) + jnp.bitwise_and(a5, 7)).astype(F32)
    code5 = sq_ref[0:16, :]
    code5 = jnp.where(live(c5_ref, 16), code5, -1.0)
    sq_ref[0:2, 0:NO] = (block(a4_ref[...], 1) + 32).astype(F32)
    code4 = sq_ref[0:16, :]
    code4 = jnp.where(live(c4_ref, 16), code4, -1.0)
    code = jnp.concatenate([code5, code4], axis=0)
    upper = code >= 256.0
    low54_ref[...] = jnp.where(upper, code - 256.0, code).astype(BF)
    hi54_ref[...] = upper.astype(F32).astype(BF)
    sq_ref[...] = jnp.full((R, R), -1.0, F32)
    sq_ref[0:16, 0:NO] = t5_ref[...].astype(F32)
    sq_ref[16:18, 0:NO] = t4_ref[...].astype(F32) + 32.0
    sq_ref[...] = sq_ref[...].T
    packed = sq_ref[pl.ds(0, 24, stride=4), :]
    lane = iota((24, R), 1)
    for i in range(1, 4):
        part = pltpu.roll(sq_ref[pl.ds(i, 24, stride=4), :], 32 * i, 1)
        packed = jnp.where(lane >= 32 * i, part, packed)
    t54_ref[...] = packed
    for fetch in fetches[-3:]:
        fetch.wait()


def hot(column, rows):
    wide = jnp.broadcast_to(column, (rows, R))
    lane = iota((rows, R), 1)
    one = jnp.ones((rows, R), BF)
    zero = jnp.zeros((rows, R), BF)
    left = jnp.where(wide == lane.astype(BF), one, zero)
    right = jnp.where(wide == (lane + R).astype(BF), one, zero)
    return jnp.concatenate([left, right], axis=1)


def placing(row, rows):
    wide = jnp.broadcast_to(row, (rows, R)).astype(BF)
    down = iota((rows, R), 0).astype(BF)
    return jnp.where(wide == down, jnp.ones((rows, R), BF), jnp.zeros((rows, R), BF))


def fine_kernel(z_ref, g_ref, own_ref, prev_ref, next_ref, far_ref, t_ref, low_ref, hi_ref, tgt_ref, acc_ref, x_ref):
    z = z_ref[0]
    x_ref[:, R : 2 * R] = own_ref[0:256]

    g = g_ref[0]
    nothing = jnp.zeros((256, R), BF)

    @pl.when(z == 0)
    def _():
        x_ref[:, 0:R] = jnp.where(g > 0, far_ref[...], nothing)

    @pl.when(z > 0)
    def _():
        x_ref[:, 0:R] = prev_ref[0:256]

    @pl.when(z == 7)
    def _():
        x_ref[:, 2 * R : 3 * R] = jnp.where(g < 7, far_ref[...], nothing)

    @pl.when(z < 7)
    def _():
        x_ref[:, 2 * R : 3 * R] = next_ref[0:256]

    low = low_ref[...]
    hi = hi_ref[...]
    for first in range(0, NO, G):
        ops = range(first, min(first + G, NO))
        hots = jnp.concatenate([hot(low[:, o : o + 1], R) for o in ops], axis=0)
        found = jnp.dot(hots, x_ref[...], preferred_element_type=F32).astype(BF)
        ys, places = [], []
        for n, o in enumerate(ops):
            seg = jnp.broadcast_to(hi[:, o : o + 1], (R, R))
            p = found[n * R : (n + 1) * R]
            p = jnp.where(seg == jnp.asarray(0, BF), p[:, 0:R], jnp.where(seg == jnp.asarray(1, BF), p[:, R : 2 * R], p[:, 2 * R :]))
            ys.append(jnp.dot(p, t_ref[o], preferred_element_type=F32).astype(BF))
            places.append(placing(tgt_ref[o : o + 1, :], 256))
        added = jnp.dot(jnp.concatenate(places, axis=1), jnp.concatenate(ys, axis=0), preferred_element_type=F32)
        if first == 0:
            acc_ref[...] = added
        else:
            acc_ref[...] += added


def coarse_kernel(q_ref, acc_ref, both_ref, prev_ref, next_ref, p_ref, m_ref, t_ref, low_ref, hi_ref, t54_ref,
                  o0_ref, o1_ref, o2_ref, o3_ref, x_ref, far_ref):
    x_ref[0:48, 0:R] = both_ref[256:304]
    x_ref[48:96, 0:R] = next_ref[256:304]
    x_ref[96:144, 0:R] = m_ref[48:96]
    x_ref[144:192, 0:R] = m_ref[0:48]
    x_ref[0:48, R : 2 * R] = m_ref[96:144]
    x_ref[48:96, R : 2 * R] = p_ref[0:48]
    x_ref[96:144, R : 2 * R] = p_ref[48:96]
    x_ref[144:192, R : 2 * R] = prev_ref[256:304]
    x_ref[192:256, :] = jnp.zeros((64, 2 * R), BF)
    low = low_ref[...]
    hi = hi_ref[...]
    for first in range(0, NO, NO):
        ops = range(first, min(first + NO, NO))
        hots = jnp.concatenate([hot(low[:, o : o + 1], 32) for o in ops], axis=0)
        found = jnp.dot(hots, x_ref[...], preferred_element_type=F32).astype(BF)
        ys = []
        for n, o in enumerate(ops):
            seg = jnp.broadcast_to(hi[:, o : o + 1], (32, R))
            p = found[n * 32 : (n + 1) * 32]
            p = jnp.where(seg == jnp.asarray(0, BF), p[:, 0:R], p[:, R:])
            ys.append(jnp.dot(p, t_ref[o], preferred_element_type=F32).astype(BF))
        short = -len(ops) % 4
        if short:
            ys.append(jnp.zeros((32 * short, R), BF))
        rows = range(first // 4, (first + len(ops) + 3) // 4)
        places = jnp.concatenate([placing(t54_ref[j : j + 1, :], 48) for j in rows], axis=1)
        added = jnp.dot(places, jnp.concatenate(ys, axis=0), preferred_element_type=F32)
        if first == 0:
            far_ref[...] = added
        else:
            far_ref[...] += added
    q = q_ref[0]
    far_ref[0:32] = far_ref[0:32] * 0.5
    far_ref[32:48] = far_ref[32:48] * 0.25
    for k, out in enumerate((o0_ref, o1_ref, o2_ref, o3_ref)):
        d = jnp.bitwise_xor(q, k)
        out[0:64] = acc_ref[pl.ds(64 * d, 64), :].astype(BF)
        five = far_ref[pl.ds(8 * d, 8), :]
        four = jnp.broadcast_to(far_ref[pl.ds(32 + d, 1), :], (8, R))
        small = jnp.concatenate([five, four], axis=0)
        top = small.astype(BF)
        out[64:80] = top


def final_kernel(a_ref, b_ref, c_ref, d_ref, dn_ref, out_ref, s_ref):
    total = (a_ref[...].astype(F32) + b_ref[...].astype(F32)) + (c_ref[...].astype(F32) + d_ref[...].astype(F32))
    small = total[64:80]
    far5 = small[0:8]
    local4 = small[8:16].astype(BF)
    row = iota((8, R), 0)
    local5 = far5
    for c in range(8):
        spread = jnp.dot(local4, dn_ref[c], preferred_element_type=F32)
        local5 = local5 + jnp.where(row == c, spread, 0.0)
    local5 = local5.astype(BF)
    for c in range(8):
        s_ref[pl.ds(c, 8, stride=8), :] = jnp.dot(local5, dn_ref[c], preferred_element_type=F32)
    out_ref[...] = (total[0:64] + s_ref[...]).astype(BF)


VM = pl.BlockSpec(memory_space=pltpu.VMEM)
SM = pl.BlockSpec(memory_space=pltpu.SMEM)
FAR = pl.BlockSpec(memory_space=pl.ANY)
LIMIT = pltpu.CompilerParams(vmem_limit_bytes=24 * 1024 * 1024)


def near_core(value):
    return pltpu.with_memory_space_constraint(value, pltpu.VMEM)


def in_hbm(value):
    return pltpu.with_memory_space_constraint(value, pltpu.HBM)


def call(kernel, outs, scratch, vectors, scalars=(), far=0):
    return pl.pallas_call(
        kernel,
        out_shape=tuple(pltpu.VMEM(dims, kind) for dims, kind in outs),
        in_specs=[SM] * len(scalars) + [VM] * (len(vectors) - far) + [FAR] * far,
        out_specs=tuple([VM] * len(outs)),
        scratch_shapes=scratch,
        compiler_params=LIMIT,
    )(*scalars, *vectors)


SUB = ("x", "c")
MORTON = ("g", "z")


def rows_of(table):
    return table.transpose(1, 0, 2)


def crossed(value, k):
    return lax.ppermute(value, SUB, [(i, i ^ k) for i in range(4)])


def local(multipoles, translations, upward_ops, downward_ops, targets_l6, source_boxes_level6, counts_l6,
          target_boxes_level5, anchors_l5, counts_l5, targets_l4, anchors_l4, counts_l4):
    q = lax.axis_index(SUB).astype(jnp.int32).reshape(1)
    z = lax.axis_index("z").astype(jnp.int32).reshape(1)
    g = lax.axis_index("g").astype(jnp.int32).reshape(1)
    groups, ring = lax.axis_size("g"), lax.axis_size("z")
    ends = [(i * ring + ring - 1, i * ring + ring) for i in range(groups - 1)]
    ends = dict(ends + [(j, i) for i, j in ends])

    peers = []
    for k in (1, 2, 3):
        peers.append(crossed(multipoles, k))
    low6, hi6, low54, hi54, t54, tgt, mine, up, held = call(
        prep_kernel,
        [((R, R), BF), ((R, R), BF), ((32, R), BF), ((32, R), BF), ((24, R), F32), ((80, R), F32),
         ((64, R), BF), ((8, R, R), BF), ((NO, R, R), BF)],
        [pltpu.VMEM((R, R), F32),
         pltpu.VMEM((NO, 1, R), jnp.int32), pltpu.VMEM((1, NO), jnp.int32), pltpu.VMEM((16, NO), jnp.int32),
         pltpu.VMEM((1, NO), jnp.int32), pltpu.VMEM((2, NO), jnp.int32), pltpu.VMEM((1, NO), jnp.int32),
         pltpu.VMEM((16, NO), jnp.int32), pltpu.VMEM((2, NO), jnp.int32), pltpu.VMEM((NO, 1, R), jnp.int32),
         pltpu.SemaphoreType.DMA((12,))],
        [*map(in_hbm, (multipoles, upward_ops, rows_of(source_boxes_level6), counts_l6, anchors_l5[0].T, counts_l5,
                       anchors_l4[0].T, counts_l4, target_boxes_level5[0].T, targets_l4[0].T, rows_of(targets_l6), translations))],
        [4 * z + q], far=12)
    (both,) = call(upward_kernel, [((304, R), BF)], [pltpu.VMEM((256, R), F32), pltpu.VMEM((32, R), F32)],
                   [*map(near_core, (mine, *peers, up))])

    def shifted(value, by):
        return lax.ppermute(value, "z", [(i, (i + by) % ring) for i in range(ring)])

    before = shifted(both, 1)
    after = shifted(both, -1)
    far = lax.ppermute(both[0:256], MORTON, [(i, ends.get(i, i)) for i in range(groups * ring)])
    pair = jnp.concatenate([both[256:304], after[256:304]], axis=0)
    three = jnp.concatenate([both[256:304], before[256:304], after[256:304]], axis=0)
    minus = shifted(three, -3)
    plus = shifted(pair, 3)
    (fine,) = call(fine_kernel, [((256, R), F32)], [pltpu.VMEM((256, 3 * R), BF)],
                   [*map(near_core, (both, before, after, far, held, low6, hi6, tgt))], [z, g])
    parts = call(coarse_kernel, [((80, R), BF)] * 4, [pltpu.VMEM((256, 2 * R), BF), pltpu.VMEM((48, R), F32)],
                 [*map(near_core, (fine, both, before, after, plus, minus, held, low54, hi54, t54))], [q])
    received = []
    for k in (1, 2, 3):
        received.append(crossed(parts[k], k))
    return pl.pallas_call(
        final_kernel,
        out_shape=jax.ShapeDtypeStruct((64, R), BF),
        in_specs=[VM] * 5,
        out_specs=VM,
        scratch_shapes=[pltpu.VMEM((64, R), F32)],
        compiler_params=LIMIT,
        name="downward",
    )(*[near_core(v) for v in (parts[0], *received, downward_ops)])


def solution(mesh):
    cut = Mesh(mesh.devices.reshape(8, 8, 2, 2), ("g", "z", "x", "c"))
    both = MORTON + SUB
    placed = (
        P(both, None),
        P(SUB, None, None),
        P(),
        P(),
        P(MORTON, SUB, None),
        P(MORTON, SUB, None),
        P(MORTON, SUB),
        P(MORTON, SUB, None),
        P(MORTON, SUB, None),
        P(MORTON, SUB),
        P(MORTON, SUB, None),
        P(MORTON, SUB, None),
        P(MORTON, SUB),
    )
    return jax.shard_map(local, mesh=cut, in_specs=placed, out_specs=P(both, None), check_vma=False)
```
